32 devices in a mesh: ctx: 4 (over z), seq: 2 (over y), head: 4 (over x, core).
Axes of the slice: x: 2, y: 2, z: 4, core: 2. Of those that a mesh axis runs over, the one named last changes fastest.
Arguments:
- queries: bfloat16 [1536, 2560], P(('ctx', 'seq'), 'head'), may hold values from -7 to 7
- key_rows: bfloat16 [1536, 512], P(('ctx', 'seq'), 'head'), may hold values from -6 to 6
- value_rows: bfloat16 [1536, 512], P(('ctx', 'seq'), 'head'), may hold values from -12 to 12
- residual: bfloat16 [1536, 5120], P(('ctx', 'seq'), 'head'), may hold values from -4 to 4
- norm_gain: float32 [5120], replicated, may hold values from 0.25 to 1.75
- w_out: bfloat16 [640, 8, 2560], P(None, ('ctx', 'seq'), 'head'), may hold values from -0.125 to 0.125
- student_proj: bfloat16 [5120, 2048], P(('ctx', 'seq'), 'head'), may hold values from -0.078125 to 0.078125
- target: bfloat16 [144, 8, 2048], P(None, ('ctx', 'seq'), 'head'), may hold values from -6 to 6
- span_ids: int32 [1536], P(('ctx', 'seq')), may hold values from 0 to 1151, never falling along the last dimension, each value on 1 to 3 neighbouring positions
Outputs:
- token_grads: bfloat16 [1536, 2048], P(('ctx', 'seq'), 'head')
The draws below stay inside these ranges and needn't reach their ends.
Inputs may be any that keep to these rules, and one draw needn't show every extreme that they name: span_ids never falls along the pack; every student token 0 to 1151 covers 1 to 3 consecutive teacher tokens, one exactly 3.
All inputs are finite; a program needn't handle non-finite values.
Results may differ from the reference program's by a relative error of at most 0.013.
Values may be sent and summed in bfloat16 or wider, within the bound.
A program may use at most 64 MiB of HBM per device.

```python
import math
import jax
import jax.numpy as jnp
import numpy as np
from jax import lax

D = 5120
QH = 20
KVH = 4
HD = 128
SD = 2048
TOK_DEV = 192
MOST = 3
STOPS = 2
OWNERS = 8
STU_DEV = 144
TOKENS = 1536
STUDENTS = 1152
WIN = 384


def drawn_pair(key):
    query_base = jnp.clip(1.3 * jax.random.normal(jax.random.fold_in(key, 101), (TOKENS, QH * HD), jnp.float32), -6.0, 6.0)
    key_base = jnp.clip(1.3 * jax.random.normal(jax.random.fold_in(key, 202), (TOKENS, KVH * HD), jnp.float32), -6.0, 6.0)
    return (query_base, key_base)


def draw_queries(key, part):
    return drawn_pair(key)[0].astype(jnp.bfloat16)


def draw_key_rows(key, part):
    return drawn_pair(key)[1].astype(jnp.bfloat16)


def draw_residual(key, part):
    column_pos = jnp.arange(D, dtype=jnp.float32) / D
    offset = jax.random.uniform(jax.random.fold_in(key, 21), (), jnp.float32)
    roughness = jax.random.uniform(jax.random.fold_in(key, 22), (D,), jnp.float32)
    column_scale = 10.0 ** (jnp.mod(column_pos + offset, 1.0) - 1.0) * (1.0 + 0.5 * roughness)
    row_scale = 10.0 ** (-jax.random.uniform(jax.random.fold_in(key, 23), (TOKENS, 1), jnp.float32))
    base_values = jnp.clip(jax.random.normal(jax.random.fold_in(key, 24), (TOKENS, D), jnp.float32), -2.5, 2.5)
    return jnp.clip(base_values * row_scale * column_scale[None, :], -4.0, 4.0).astype(jnp.bfloat16)


def block_levels(own_key, shape, cuts, smallest, high):
    loudness, own = 1.0, jax.random.fold_in(own_key, 6)
    for axis_at, parts in cuts:
        heights = jnp.exp(jax.random.uniform(jax.random.fold_in(own, axis_at), (parts,), jnp.float32, smallest / len(cuts), high / len(cuts)))
        loudness = loudness * jnp.repeat(heights, shape[axis_at] // parts).reshape([-1 if axis == axis_at else 1 for axis in range(len(shape))])
    return loudness


def profile(count, total, most, slope):
    weights = [(1 << 20) // math.isqrt(grade ** slope) + 1 for grade in range(2, count + 1)]
    spare, given = total - most - (count - 1), [1] * (count - 1)
    while spare > 0:
        movable = [i for i in range(count - 1) if given[i] < most]
        mass, left = sum([weights[i] for i in movable]), spare
        for i in movable:
            more = min(most - given[i], max(1, left * weights[i] // mass), spare)
            given[i] = given[i] + more
            spare = spare - more
    return np.array([most] + given)


def ragged_sizes(rng, count, total, reach, skew):
    if count == 2:
        one = jax.random.randint(rng, (), max(1, total - reach), min(reach, total - 1) + 1)
        return jnp.stack([one, total - one])
    tallies = jnp.asarray(profile(count, total, reach, skew), jnp.int32)
    couples = (count - 1) // 2
    donor, receiver = tallies[1:1 + 2 * couples:2], tallies[2:2 + 2 * couples:2]
    slack = jnp.minimum(donor - 1, reach - receiver)
    shifted = jax.random.randint(jax.random.fold_in(rng, 1), (couples,), 0, 1 << 20) % (slack + 1)
    tallies = tallies.at[1:1 + 2 * couples:2].set(donor - shifted).at[2:2 + 2 * couples:2].set(receiver + shifted)
    return tallies[jax.random.permutation(jax.random.fold_in(rng, 2), count)]


def noise(stream_key, extent, width, most, pieces=(), kind=jnp.bfloat16):
    drawn = width * jax.random.normal(stream_key, extent, jnp.float32)
    if pieces:
        drawn = drawn * block_levels(stream_key, extent, pieces, -0.22, 0.18)
    return jnp.clip(drawn, -most, most).astype(kind)


def setup_inputs(seed: int = 0) -> dict:
    key_of = jax.random.split(jax.random.key(seed), 10)
    queries = draw_queries(jax.random.fold_in(key_of[9], 71), 0)
    key_rows = draw_key_rows(jax.random.fold_in(key_of[9], 71), 0)
    value_rows = noise(key_of[2], (TOKENS, KVH * HD), 2.0, 12.0, ((0, 8), (1, 4)))
    residual = draw_residual(jax.random.fold_in(key_of[9], 71), 0)
    norm_gain = jnp.clip(1.0 + 0.15 * jax.random.normal(key_of[4], (D,), jnp.float32), 0.25, 1.75)
    w_out = noise(key_of[5], (D // OWNERS, OWNERS, QH * HD), (QH * HD) ** -0.5, 0.125, ((1, 8), (2, 4)))
    student_proj = noise(key_of[6], (D, SD), D ** -0.5, 0.078125, ((0, 8), (1, 4)))
    target = noise(key_of[7], (STU_DEV, OWNERS, SD), 1.0, 6.0, ((1, 8), (2, 4)))
    span_ids = jnp.searchsorted(jnp.cumsum(ragged_sizes(key_of[8], STUDENTS, TOKENS, MOST, 2)), jnp.arange(TOKENS), side="right").astype(jnp.int32)
    return {"queries": queries, "key_rows": key_rows, "value_rows": value_rows, "residual": residual, "norm_gain": norm_gain, "w_out": w_out, "student_proj": student_proj, "target": target, "span_ids": span_ids}


EPSILON = 1e-06

def attend(query_block, key_block, value_block, query_pos, key_pos):
    tok_rows = query_block.shape[0]
    kv_heads = key_block.shape[1] // HD
    group_size = query_block.shape[1] // HD // kv_heads
    query_grid = query_block.reshape(tok_rows, kv_heads, group_size, HD).astype(jnp.float32)
    key_grid = key_block.reshape(key_block.shape[0], kv_heads, HD).astype(jnp.float32)
    value_grid = value_block.reshape(value_block.shape[0], kv_heads, HD).astype(jnp.float32)
    scores = jnp.einsum('qhgd,khd->hgqk', query_grid, key_grid) * HD ** (-0.5)
    visible = (key_pos[None, :] <= query_pos[:, None]) & (key_pos[None, :] > query_pos[:, None] - WIN) & (key_pos[None, :] >= 0)
    scores = jnp.where(visible, scores, -1e+30)
    largest = lax.optimization_barrier(jnp.max(scores, axis=-1, keepdims=True))
    exponent = jnp.exp(scores - largest)
    probabilities = (exponent / lax.optimization_barrier(jnp.sum(exponent, axis=-1, keepdims=True))).astype(jnp.bfloat16)
    attended = jnp.einsum('hgqk,khd->qhgd', probabilities.astype(jnp.float32), value_grid)
    return attended.reshape(tok_rows, -1).astype(jnp.bfloat16)

def reference(queries, key_rows, value_rows, residual, norm_gain, w_out, student_proj, target, span_ids):
    window_reach = STOPS * TOK_DEV
    front_zeros = jnp.zeros((window_reach, key_rows.shape[1]), jnp.bfloat16)
    keys_padded = jnp.concatenate([front_zeros, key_rows], axis=0)
    values_padded = jnp.concatenate([front_zeros, value_rows], axis=0)

    def one_block(block_index):
        first_row = (block_index * TOK_DEV).astype(jnp.int32)
        query_block = lax.dynamic_slice_in_dim(queries, first_row, TOK_DEV, 0)
        key_block = lax.dynamic_slice_in_dim(keys_padded, first_row, window_reach + TOK_DEV, 0)
        value_block = lax.dynamic_slice_in_dim(values_padded, first_row, window_reach + TOK_DEV, 0)
        query_pos = first_row + jnp.arange(TOK_DEV, dtype=jnp.int32)
        key_pos = first_row - window_reach + jnp.arange(window_reach + TOK_DEV, dtype=jnp.int32)
        return attend(query_block, key_block, value_block, query_pos, key_pos)
    attended = lax.map(one_block, jnp.arange(TOKENS // TOK_DEV, dtype=jnp.int32)).reshape(TOKENS, QH * HD)
    out_matrix = w_out.reshape(D, QH * HD)
    product = lax.dot_general(attended, out_matrix, (((1,), (1,)), ((), ())), preferred_element_type=jnp.float32)
    summed = residual.astype(jnp.float32) + product
    mean_square = lax.optimization_barrier(jnp.mean(summed * summed, axis=1, keepdims=True))
    normed = (summed * lax.rsqrt(mean_square + EPSILON) * norm_gain[None, :]).astype(jnp.bfloat16)
    projected = jnp.dot(normed, student_proj, preferred_element_type=jnp.float32)
    unit_weights = jnp.ones((TOKENS,), jnp.float32)
    counts = jax.ops.segment_sum(unit_weights, span_ids, num_segments=STUDENTS)
    span_sums = jax.ops.segment_sum(projected, span_ids, num_segments=STUDENTS)
    pooled = span_sums / counts[:, None]
    target_rows = target.astype(jnp.float32).reshape(STUDENTS, SD)
    student_grads = ((pooled - target_rows) / counts[:, None]).astype(jnp.bfloat16)
    return student_grads[span_ids]
```

```python
import functools

import jax
import jax.numpy as jnp
from jax import lax
from jax.experimental import pallas as pl
from jax.experimental.pallas import tpu as pltpu
from jax.sharding import PartitionSpec as P

D = 5120
HD = 128
STOPS = 2
WIN = 384


EPSILON = 1e-06


def passed_along(value, axis, steps):
    count = lax.axis_size(axis)
    first, last = (max(0, -steps), min(count, count - steps))
    return lax.ppermute(value, axis, [(source, source + steps) for source in range(first, last)])


def attend(queries, keys_all, values_all, query_pos, key_pos):
    tok_rows = queries.shape[0]
    kv_heads = keys_all.shape[1] // HD
    group_size = queries.shape[1] // HD // kv_heads
    query_blocks = queries.reshape(tok_rows, kv_heads, group_size, HD)
    key_blocks = keys_all.reshape(keys_all.shape[0], kv_heads, HD)
    value_blocks = values_all.reshape(values_all.shape[0], kv_heads, HD)
    scores = jnp.einsum(
        "qhgd,khd->hgqk", query_blocks, key_blocks, preferred_element_type=jnp.float32
    ) * HD ** (-0.5)
    visible = (
        (key_pos[None, :] <= query_pos[:, None])
        & (key_pos[None, :] > query_pos[:, None] - WIN)
        & (key_pos[None, :] >= 0)
    )
    scores = jnp.where(visible, scores, -1e30)
    largest = jnp.max(scores, axis=-1, keepdims=True)
    exponent = jnp.exp(scores - largest)
    probabilities = (exponent / jnp.sum(exponent, axis=-1, keepdims=True)).astype(jnp.bfloat16)
    attended = jnp.einsum(
        "hgqk,khd->qhgd", probabilities, value_blocks, preferred_element_type=jnp.float32
    )
    return attended.reshape(tok_rows, -1).astype(jnp.bfloat16)


def per_device(
    queries, key_rows, value_rows, residual, norm_gain, w_out, student_proj, target, span_ids
):
    tok_rows = queries.shape[0]
    block_index = lax.axis_index(("ctx", "seq"))
    owners = lax.axis_size(("ctx", "seq"))
    stacked = jnp.stack([key_rows, value_rows])
    arrived = []
    moving = stacked
    for back_step in range(STOPS):
        moving = passed_along(moving, ("ctx", "seq"), 1)
        arrived.append(moving)
    ordered = jnp.concatenate(arrived[::-1] + [stacked], axis=1)
    query_pos = block_index * tok_rows + jnp.arange(tok_rows, dtype=jnp.int32)
    key_pos = (block_index - STOPS) * tok_rows + jnp.arange((STOPS + 1) * tok_rows, dtype=jnp.int32)
    attended = attend(queries, ordered[0], ordered[1], query_pos, key_pos)
    w_source = lax.all_to_all(w_out, "head", split_axis=0, concat_axis=2, tiled=True)
    w_slab, p_slab = (
        lax.all_gather(w_source, ("ctx", "seq"), axis=1, tiled=True),
        lax.all_gather(student_proj, ("ctx", "seq"), axis=0, tiled=True),
    )
    w_slab = w_slab.reshape(-1, w_slab.shape[2])
    col_width = residual.shape[1]
    col_offset = lax.axis_index("head") * col_width
    gain_cols = lax.dynamic_slice_in_dim(norm_gain, col_offset, col_width, 0)
    all_heads = lax.all_gather(attended, "head", axis=1, tiled=True)
    share_cols = lax.dot_general(
        all_heads, w_slab, (((1,), (1,)), ((), ())), preferred_element_type=jnp.float32
    ) + residual.astype(jnp.float32)
    squares = lax.psum(jnp.sum(share_cols * share_cols, axis=1), "head")
    scaled = (share_cols * lax.rsqrt(squares / D + EPSILON)[:, None] * gain_cols[None, :]).astype(
        jnp.bfloat16
    )
    normed = lax.all_gather(scaled, "head", axis=1, tiled=True)
    projected = jnp.dot(normed, p_slab, preferred_element_type=jnp.float32)
    first_id = span_ids[0]
    slot_count = -(-tok_rows // owners)
    owner_iota = lax.broadcasted_iota(jnp.int32, (owners, slot_count), 0)
    slot_iota = lax.broadcasted_iota(jnp.int32, (owners, slot_count), 1)
    slot_ids = first_id + (owner_iota - first_id) % owners + slot_iota * owners
    slot_flat = slot_ids.reshape(-1)
    membership = (slot_flat[:, None] == span_ids[None, :]).astype(jnp.float32)
    pooled = jnp.dot(
        membership, projected, precision=lax.Precision.HIGHEST, preferred_element_type=jnp.float32
    )
    token_counts = jnp.sum(membership, axis=1)
    target_rows = (slot_flat // owners).astype(jnp.float32)
    local_cols = projected.shape[1]
    pooled_send = pooled.reshape(owners, slot_count, local_cols)
    counts_send = token_counts.reshape(owners, slot_count)
    rows_send = target_rows.reshape(owners, slot_count)
    got_sums, got_counts, got_rows = (
        lax.all_to_all(
            pooled_send.astype(jnp.bfloat16),
            ("ctx", "seq"),
            split_axis=0,
            concat_axis=0,
            tiled=True,
        ).astype(pooled_send.dtype),
        lax.all_to_all(
            counts_send.astype(jnp.bfloat16),
            ("ctx", "seq"),
            split_axis=0,
            concat_axis=0,
            tiled=True,
        ).astype(counts_send.dtype),
        lax.all_to_all(
            rows_send.astype(jnp.bfloat16), ("ctx", "seq"), split_axis=0, concat_axis=0, tiled=True
        ).astype(rows_send.dtype),
    )
    stu_rows = target.shape[0]
    row_iota = jnp.arange(stu_rows, dtype=jnp.float32)
    assign = (got_rows.reshape(-1)[None, :] == row_iota[:, None]).astype(jnp.float32)
    span_sums = jnp.dot(
        assign,
        got_sums.reshape(owners * slot_count, local_cols),
        precision=lax.Precision.HIGHEST,
        preferred_element_type=jnp.float32,
    )
    span_counts = jnp.dot(
        assign,
        got_counts.reshape(-1),
        precision=lax.Precision.HIGHEST,
        preferred_element_type=jnp.float32,
    )
    pooled_mean = span_sums / span_counts[:, None]
    grad_rows = ((pooled_mean - target[:, 0, :].astype(jnp.float32)) / span_counts[:, None]).astype(
        jnp.bfloat16
    )
    returned = lax.dot_general(
        assign.astype(jnp.bfloat16),
        grad_rows,
        (((0,), (0,)), ((), ())),
        preferred_element_type=jnp.float32,
    ).astype(jnp.bfloat16)
    returned = returned.reshape(owners, slot_count, local_cols)
    back_rows = lax.all_to_all(returned, ("ctx", "seq"), split_axis=0, concat_axis=0, tiled=True)
    back_rows = back_rows.reshape(owners * slot_count, local_cols)
    token_grads = lax.dot_general(
        membership.astype(jnp.bfloat16),
        back_rows,
        (((0,), (0,)), ((), ())),
        preferred_element_type=jnp.float32,
    )
    return token_grads.astype(jnp.bfloat16)


BF16 = jnp.bfloat16
F32 = jnp.float32
MESH = pl.DeviceIdType.MESH
EDGE = 8


def mm(a, b):
    return jnp.dot(a, b, preferred_element_type=F32)


def fused_kernel(
    Z, Y, H, q_ref, k_ref, v_ref, res_ref, gain_ref, w_ref, proj_ref, tgt_ref, idr_ref, idc_ref,
    out_ref,
    kbuf, vbuf, att, attbuf, wbuf, wnat, projbuf, resbuf, s1, r1, s2, r2, nbuf, ssbuf, sst, ssall,
    psend, pbuf, idbuf, tsend, tbuf, ebuf, edge_prev, edge_next,
    send_sem, recv_sem, res_send, res_recv,
):
    z, y, h = lax.axis_index("ctx"), lax.axis_index("seq"), lax.axis_index("head")
    core, xpos = h % 2, h // 2
    mate = h + 1 - 2 * core
    cross = (h + 2) % H
    other_y = 1 - y
    owners = Z * Y
    me = z * Y + y
    T = q_ref.shape[0]
    F = gain_ref.shape[1] // Z
    half, quarter = T // 2, T // 4

    barrier = pltpu.get_barrier_semaphore()
    count = 0
    for dz in range(Z):
        for dh in range(H):
            if dz or dh:
                pl.semaphore_signal(
                    barrier, inc=1, device_id=((z + dz) % Z, y, (h + dh) % H), device_id_type=MESH
                )
                count += 1
        pl.semaphore_signal(
            barrier, inc=1, device_id=((z + dz) % Z, other_y, h), device_id_type=MESH
        )
        count += 1
    pl.semaphore_wait(barrier, count)

    sends = []

    def send(source, dest, device):
        n = len(sends)
        copy = pltpu.make_async_remote_copy(
            src_ref=source, dst_ref=dest, send_sem=send_sem.at[n], recv_sem=recv_sem.at[n],
            device_id=device, device_id_type=MESH,
        )
        copy.start()
        sends.append(copy)
        return copy

    def owner(step):
        block = (me + step + owners) % owners
        return (block // Y, block % Y, h)

    def rows_of(head):
        return pl.multiple_of((head % 2) * half + (head // 2) * quarter, 16)

    halo = []
    for step in range(1, STOPS + 1):
        halo.append(send(k_ref, kbuf.at[STOPS - step], owner(step)))
        halo.append(send(v_ref, vbuf.at[STOPS - step], owner(step)))
    ids_in = [send(idr_ref, idbuf.at[k], owner(k)) for k in range(1, owners)]

    wrows = w_ref.shape[0] // Z

    def w_chunk(block):
        return w_ref.at[pl.ds(pl.multiple_of(block * wrows, 16), wrows)]

    w_z = [send(w_chunk((z + m) % Z), wbuf.at[me], ((z + m) % Z, y, h)) for m in range(1, Z)]
    w_y = [send(w_chunk(z), wbuf.at[me], (z, other_y, h))]
    wbuf[me] = w_chunk(z)[...]

    res_slot = (h - z + Z) % Z
    res_copies = []
    for n in range(H):
        hh = (h + n) % H
        copy = pltpu.make_async_remote_copy(
            src_ref=res_ref.at[pl.ds(rows_of(hh), quarter)], dst_ref=resbuf.at[res_slot],
            send_sem=res_send.at[n], recv_sem=res_recv.at[res_slot],
            device_id=(h, y, hh), device_id_type=MESH,
        )
        res_copies.append(copy)

    local = pltpu.make_async_copy(
        res_ref.at[pl.ds(rows_of(h), quarter)], resbuf.at[0], res_recv.at[0]
    )

    slots = tbuf.shape[1]
    students = tgt_ref.shape[0]
    shift = owners.bit_length() - 1

    def choose():
        for k in range(1, owners):
            ids_in[k - 1].wait_recv()
        slot = lax.broadcasted_iota(jnp.int32, (slots, students), 0)
        row = lax.broadcasted_iota(jnp.int32, (slots, students), 1)
        for k in range(owners):
            ids = idr_ref[0:1, 0:1] if k == 0 else idbuf[k, 0:1, 0:1]
            dist = row * owners + me - ids
            pick = ((dist >= slot * owners) & (dist < slot * owners + owners)).astype(F32)
            rows = mm(pick.astype(BF16), tgt_ref[...]).astype(BF16)
            if k == 0:
                tbuf[0] = rows
            else:
                tsend[k] = rows
        return [send(tsend.at[k], tbuf.at[k], owner(-k)) for k in range(1, owners)]

    targets_in = choose()

    for copy in halo:
        copy.wait_recv()
    keys = jnp.concatenate([kbuf[s] for s in range(STOPS)] + [k_ref[...]], axis=0)
    values = jnp.concatenate([vbuf[s] for s in range(STOPS)] + [v_ref[...]], axis=0)
    span = (STOPS + 1) * T
    qpos = lax.broadcasted_iota(jnp.int32, (T, span), 0) + STOPS * T
    kpos = lax.broadcasted_iota(jnp.int32, (T, span), 1)
    visible = (kpos <= qpos) & (kpos > qpos - WIN) & (kpos >= (STOPS - me) * T)
    for g in range(q_ref.shape[1] // HD):
        scores = lax.dot_general(
            q_ref[:, g * HD:(g + 1) * HD], keys, (((1,), (1,)), ((), ())),
            preferred_element_type=F32,
        ) * HD ** (-0.5)
        scores = jnp.where(visible, scores, -1e30)
        exponent = jnp.exp(scores - jnp.max(scores, axis=-1, keepdims=True))
        inverse = 1.0 / jnp.sum(exponent, axis=-1, keepdims=True)
        att[:, g * HD:(g + 1) * HD] = mm((exponent * inverse).astype(BF16), values).astype(BF16)
    att_in = [send(att, attbuf.at[m], ((z + m) % Z, y, h)) for m in range(1, Z)]

    for n in range(1, H):
        res_copies[n].start()

    @pl.when(z != h)
    def _():
        res_copies[0].start()

    @pl.when(z == h)
    def _():
        local.start()

    for m in range(1, Z):
        w_z[m - 1].wait_recv()
        slot = ((z - m + Z) % Z) * Y + y
        w_y.append(send(wbuf.at[slot], wbuf.at[slot], (z, other_y, h)))
    proj_in = send(proj_ref, projbuf.at[y], (z, other_y, h))
    projbuf[y] = proj_ref[...]
    for copy in w_y:
        copy.wait_recv()

    group = 128 // owners
    r_io = lax.broadcasted_iota(jnp.int32, (128, 128), 0)
    c_io = lax.broadcasted_iota(jnp.int32, (128, 128), 1)
    place = ((r_io & (group - 1)) * owners + (r_io >> (group.bit_length() - 1)) == c_io).astype(F32).astype(BF16)
    for k in range(F // 128):
        rows = jnp.concatenate([wbuf[o, k * group:(k + 1) * group] for o in range(owners)], axis=0)
        wnat[:, k * 128:(k + 1) * 128] = lax.dot_general(
            rows, place, (((0,), (0,)), ((), ())), preferred_element_type=F32
        ).astype(BF16)

    gain = gain_ref[:, pl.ds(pl.multiple_of(z * F, 128), F)]
    mine, his = pl.multiple_of(core * half, 16), pl.multiple_of((1 - core) * half, 16)
    own_quarter = pl.multiple_of(xpos * quarter, 16)
    his_quarter = pl.multiple_of((1 - xpos) * quarter, 16)
    at_mine = rows_of(h)
    at_cross = rows_of(cross)
    first, second, third, mates, ss_in, p_in = [], [], [], [], [], []

    def stage_a(m):
        if m:
            att_in[m - 1].wait_recv()
        source = att if m == 0 else attbuf.at[m]
        s1[m] = mm(source[pl.ds(his, half)], wnat[...]).astype(BF16)
        first.append(send(s1.at[m], r1.at[m], (z, y, mate)))

    def stage_b(m):
        source = att if m == 0 else attbuf.at[m]
        mine_a = mm(source[pl.ds(pl.multiple_of(mine + his_quarter, 16), quarter)], wnat[...])
        first[m].wait_recv()
        s2[m] = (mine_a + r1[m, pl.ds(his_quarter, quarter)].astype(F32)).astype(BF16)
        second.append(send(s2.at[m], r2.at[m], (z, y, cross)))

    def stage_c(m):
        source = att if m == 0 else attbuf.at[m]
        total = mm(source[pl.ds(at_mine, quarter)], wnat[...])
        total = total + r1[m, pl.ds(own_quarter, quarter)].astype(F32)
        pltpu.make_async_copy(resbuf.at[m], resbuf.at[m], res_recv.at[m]).wait()
        second[m].wait_recv()
        total = total + r2[m].astype(F32) + resbuf[m].astype(F32)
        nbuf[m, pl.ds(at_mine, quarter)] = (total * gain).astype(BF16)
        block = nbuf.at[m, pl.ds(at_mine, quarter)]
        third.append(send(block, block, (z, y, cross)))
        mates.append([send(block, block, (z, y, mate))])
        squares = jnp.sum(total * total, axis=1, keepdims=True)
        squares = jnp.broadcast_to(squares, (quarter, 128))
        if m == 0:
            ssbuf[0] = squares
        else:
            sst[m] = squares
            ss_in.append(send(sst.at[m], ssbuf.at[m], ((z - m + Z) % Z, y, h)))

    def stage_d(m):
        third[m].wait_recv()
        block = nbuf.at[m, pl.ds(at_cross, quarter)]
        mates[m].append(send(block, block, (z, y, mate)))

    def stage_e(m):
        for copy in mates[m]:
            copy.wait_recv()
        if m == 0:
            proj_in.wait_recv()
        depth = F // Y
        part = mm(nbuf[m, :, 0:depth], projbuf[0])
        for s in range(1, Y):
            part = part + mm(nbuf[m, :, s * depth:(s + 1) * depth], projbuf[s])
        if m == 0:
            ebuf[...] = part
        else:
            psend[m] = part.astype(BF16)
            p_in.append(send(psend.at[m], pbuf.at[m], ((z - m + Z) % Z, y, h)))

    stage_a(0)
    stage_b(0)
    stage_c(0)
    stage_a(1)
    stage_d(0)
    stage_b(1)
    stage_e(0)
    stage_c(1)
    stage_a(2)
    stage_d(1)
    stage_b(2)
    stage_e(1)
    stage_c(2)
    stage_a(3)
    stage_d(2)
    stage_b(3)
    stage_e(2)
    stage_c(3)

    squares = ssbuf[0]
    for m in range(1, Z):
        ss_in[m - 1].wait_recv()
        squares = squares + ssbuf[m]
    ssall[pl.ds(at_mine, quarter)] = squares
    block = ssall.at[pl.ds(at_mine, quarter)]
    ss_all = [send(block, block, (z, y, (h + n) % H)) for n in range(1, H)]
    stage_d(3)
    stage_e(3)
    for copy in ss_all:
        copy.wait_recv()
    projected = ebuf[...]
    for m in range(1, Z):
        p_in[m - 1].wait_recv()
        projected = projected + pbuf[m].astype(F32)
    projected = projected * lax.rsqrt(ssall[:, 0:1] / D + EPSILON)
    ebuf[...] = projected
    after = send(ebuf.at[pl.ds(T - EDGE, EDGE)], edge_prev, owner(1))
    before = send(ebuf.at[pl.ds(0, EDGE)], edge_next, owner(-1))

    ids = idc_ref[...]
    same = (ids == idr_ref[0:1, :]).astype(F32)
    sums = jnp.dot(
        same, projected, precision=lax.Precision.HIGHEST, preferred_element_type=F32
    )
    counts = jnp.sum(same, axis=1, keepdims=True)
    for copy in targets_in:
        copy.wait_recv()
    start = idr_ref[0:1, 0:1]
    from_owner = ((ids & (owners - 1)) - me + owners) & (owners - 1)
    column = from_owner * slots + ((ids - start) >> shift)
    choice = (
        lax.broadcasted_iota(jnp.int32, (T, owners * slots), 1) == column
    ).astype(F32).astype(BF16)
    wanted = mm(choice, jnp.concatenate([tbuf[k] for k in range(owners)], axis=0))
    after.wait_recv()
    before.wait_recv()
    for u in range(MOST - 1):
        spot = EDGE - 1 - u
        hit = (ids == idbuf[1, 0:1, T - 1 - u:T - u]).astype(F32)
        sums = sums + hit * edge_prev[spot:spot + 1]
        counts = counts + hit
        hit = (ids == idbuf[owners - 1, 0:1, u:u + 1]).astype(F32)
        sums = sums + hit * edge_next[u:u + 1]
        counts = counts + hit
    out_ref[...] = ((sums / counts - wanted) / counts).astype(BF16)

    for copy in sends:
        copy.wait_send()
    for n in range(1, H):
        res_copies[n].wait_send()

    @pl.when(z != h)
    def _():
        res_copies[0].wait_send()


MOST = 3


def fused(
    sizes, queries, key_rows, value_rows, residual, norm_gain, w_out, student_proj, target, span_ids
):
    Z, Y, H = sizes
    owners = Z * Y
    T, width = queries.shape
    kv = key_rows.shape[1]
    F = residual.shape[1]
    cols = student_proj.shape[1]
    w = w_out.reshape(w_out.shape[0], w_out.shape[2])
    tgt = target.reshape(target.shape[0], target.shape[2])
    half, quarter = T // 2, T // 4
    slots = -(-(-(-T // owners)) // 16) * 16
    n_copies = 96
    ids_rows = jnp.broadcast_to(span_ids[None, :], (8, T))
    vmem = pltpu.VMEM
    call = pl.pallas_call(
        functools.partial(fused_kernel, Z, Y, H),
        out_shape=jax.ShapeDtypeStruct((T, cols), BF16),
        in_specs=[pl.BlockSpec(memory_space=pltpu.VMEM)] * 10,
        out_specs=pl.BlockSpec(memory_space=pltpu.VMEM),
        scratch_shapes=[
            vmem((STOPS, T, kv), BF16),
            vmem((STOPS, T, kv), BF16),
            vmem((T, width), BF16),
            vmem((Z, T, width), BF16),
            vmem((owners, w.shape[0] // Z, width), BF16),
            vmem((width, F), BF16),
            vmem((Y, student_proj.shape[0], cols), BF16),
            vmem((Z, quarter, F), BF16),
            vmem((Z, half, F), BF16),
            vmem((Z, half, F), BF16),
            vmem((Z, quarter, F), BF16),
            vmem((Z, quarter, F), BF16),
            vmem((Z, T, F), BF16),
            vmem((Z, quarter, 128), F32),
            vmem((Z, quarter, 128), F32),
            vmem((T, 128), F32),
            vmem((Z, T, cols), BF16),
            vmem((Z, T, cols), BF16),
            vmem((owners, 8, T), jnp.int32),
            vmem((owners, slots, cols), BF16),
            vmem((owners, slots, cols), BF16),
            vmem((T, cols), F32),
            vmem((EDGE, cols), F32),
            vmem((EDGE, cols), F32),
            pltpu.SemaphoreType.DMA((n_copies,)),
            pltpu.SemaphoreType.DMA((n_copies,)),
            pltpu.SemaphoreType.DMA((H,)),
            pltpu.SemaphoreType.DMA((Z,)),
        ],
        compiler_params=pltpu.CompilerParams(
            collective_id=0, has_side_effects=True, vmem_limit_bytes=60 * 2**20
        ),
        name="layer",
    )
    return call(
        queries, key_rows, value_rows, residual, norm_gain.reshape(1, -1), w, student_proj, tgt,
        ids_rows, span_ids[:, None],
    )


def solution(mesh):
    sizes = tuple(mesh.shape[axis] for axis in ("ctx", "seq", "head"))
    owners = sizes[0] * sizes[1]
    small = sizes[1] == 2 and sizes[0] == 4 and sizes[2] == 4
    body = functools.partial(fused, sizes) if small else per_device
    return jax.shard_map(
        body,
        mesh=mesh,
        in_specs=(
            P(("ctx", "seq"), "head"),
            P(("ctx", "seq"), "head"),
            P(("ctx", "seq"), "head"),
            P(("ctx", "seq"), "head"),
            P(),
            P(None, ("ctx", "seq"), "head"),
            P(("ctx", "seq"), "head"),
            P(None, ("ctx", "seq"), "head"),
            P(("ctx", "seq")),
        ),
        out_specs=P(("ctx", "seq"), "head"),
        check_vma=False,
    )
```

```python
import functools

import jax
import jax.numpy as jnp
from jax import lax
from jax.experimental import pallas as pl
from jax.experimental.pallas import tpu as pltpu
from jax.sharding import PartitionSpec as P

D = 5120
HD = 128
STOPS = 2
WIN = 384


EPSILON = 1e-06


def passed_along(value, axis, steps):
    count = lax.axis_size(axis)
    first, last = (max(0, -steps), min(count, count - steps))
    return lax.ppermute(value, axis, [(source, source + steps) for source in range(first, last)])


def attend(queries, keys_all, values_all, query_pos, key_pos):
    tok_rows = queries.shape[0]
    kv_heads = keys_all.shape[1] // HD
    group_size = queries.shape[1] // HD // kv_heads
    query_blocks = queries.reshape(tok_rows, kv_heads, group_size, HD)
    key_blocks = keys_all.reshape(keys_all.shape[0], kv_heads, HD)
    value_blocks = values_all.reshape(values_all.shape[0], kv_heads, HD)
    scores = jnp.einsum(
        "qhgd,khd->hgqk", query_blocks, key_blocks, preferred_element_type=jnp.float32
    ) * HD ** (-0.5)
    visible = (
        (key_pos[None, :] <= query_pos[:, None])
        & (key_pos[None, :] > query_pos[:, None] - WIN)
        & (key_pos[None, :] >= 0)
    )
    scores = jnp.where(visible, scores, -1e30)
    largest = jnp.max(scores, axis=-1, keepdims=True)
    exponent = jnp.exp(scores - largest)
    probabilities = (exponent / jnp.sum(exponent, axis=-1, keepdims=True)).astype(jnp.bfloat16)
    attended = jnp.einsum(
        "hgqk,khd->qhgd", probabilities, value_blocks, preferred_element_type=jnp.float32
    )
    return attended.reshape(tok_rows, -1).astype(jnp.bfloat16)


def per_device(
    queries, key_rows, value_rows, residual, norm_gain, w_out, student_proj, target, span_ids
):
    tok_rows = queries.shape[0]
    block_index = lax.axis_index(("ctx", "seq"))
    owners = lax.axis_size(("ctx", "seq"))
    stacked = jnp.stack([key_rows, value_rows])
    arrived = []
    moving = stacked
    for back_step in range(STOPS):
        moving = passed_along(moving, ("ctx", "seq"), 1)
        arrived.append(moving)
    ordered = jnp.concatenate(arrived[::-1] + [stacked], axis=1)
    query_pos = block_index * tok_rows + jnp.arange(tok_rows, dtype=jnp.int32)
    key_pos = (block_index - STOPS) * tok_rows + jnp.arange((STOPS + 1) * tok_rows, dtype=jnp.int32)
    attended = attend(queries, ordered[0], ordered[1], query_pos, key_pos)
    w_source = lax.all_to_all(w_out, "head", split_axis=0, concat_axis=2, tiled=True)
    w_slab, p_slab = (
        lax.all_gather(w_source, ("ctx", "seq"), axis=1, tiled=True),
        lax.all_gather(student_proj, ("ctx", "seq"), axis=0, tiled=True),
    )
    w_slab = w_slab.reshape(-1, w_slab.shape[2])
    col_width = residual.shape[1]
    col_offset = lax.axis_index("head") * col_width
    gain_cols = lax.dynamic_slice_in_dim(norm_gain, col_offset, col_width, 0)
    all_heads = lax.all_gather(attended, "head", axis=1, tiled=True)
    share_cols = lax.dot_general(
        all_heads, w_slab, (((1,), (1,)), ((), ())), preferred_element_type=jnp.float32
    ) + residual.astype(jnp.float32)
    squares = lax.psum(jnp.sum(share_cols * share_cols, axis=1), "head")
    scaled = (share_cols * lax.rsqrt(squares / D + EPSILON)[:, None] * gain_cols[None, :]).astype(
        jnp.bfloat16
    )
    normed = lax.all_gather(scaled, "head", axis=1, tiled=True)
    projected = jnp.dot(normed, p_slab, preferred_element_type=jnp.float32)
    first_id = span_ids[0]
    slot_count = -(-tok_rows // owners)
    owner_iota = lax.broadcasted_iota(jnp.int32, (owners, slot_count), 0)
    slot_iota = lax.broadcasted_iota(jnp.int32, (owners, slot_count), 1)
    slot_ids = first_id + (owner_iota - first_id) % owners + slot_iota * owners
    slot_flat = slot_ids.reshape(-1)
    membership = (slot_flat[:, None] == span_ids[None, :]).astype(jnp.float32)
    pooled = jnp.dot(
        membership, projected, precision=lax.Precision.HIGHEST, preferred_element_type=jnp.float32
    )
    token_counts = jnp.sum(membership, axis=1)
    target_rows = (slot_flat // owners).astype(jnp.float32)
    local_cols = projected.shape[1]
    pooled_send = pooled.reshape(owners, slot_count, local_cols)
    counts_send = token_counts.reshape(owners, slot_count)
    rows_send = target_rows.reshape(owners, slot_count)
    got_sums, got_counts, got_rows = (
        lax.all_to_all(
            pooled_send.astype(jnp.bfloat16),
            ("ctx", "seq"),
            split_axis=0,
            concat_axis=0,
            tiled=True,
        ).astype(pooled_send.dtype),
        lax.all_to_all(
            counts_send.astype(jnp.bfloat16),
            ("ctx", "seq"),
            split_axis=0,
            concat_axis=0,
            tiled=True,
        ).astype(counts_send.dtype),
        lax.all_to_all(
            rows_send.astype(jnp.bfloat16), ("ctx", "seq"), split_axis=0, concat_axis=0, tiled=True
        ).astype(rows_send.dtype),
    )
    stu_rows = target.shape[0]
    row_iota = jnp.arange(stu_rows, dtype=jnp.float32)
    assign = (got_rows.reshape(-1)[None, :] == row_iota[:, None]).astype(jnp.float32)
    span_sums = jnp.dot(
        assign,
        got_sums.reshape(owners * slot_count, local_cols),
        precision=lax.Precision.HIGHEST,
        preferred_element_type=jnp.float32,
    )
    span_counts = jnp.dot(
        assign,
        got_counts.reshape(-1),
        precision=lax.Precision.HIGHEST,
        preferred_element_type=jnp.float32,
    )
    pooled_mean = span_sums / span_counts[:, None]
    grad_rows = ((pooled_mean - target[:, 0, :].astype(jnp.float32)) / span_counts[:, None]).astype(
        jnp.bfloat16
    )
    returned = lax.dot_general(
        assign.astype(jnp.bfloat16),
        grad_rows,
        (((0,), (0,)), ((), ())),
        preferred_element_type=jnp.float32,
    ).astype(jnp.bfloat16)
    returned = returned.reshape(owners, slot_count, local_cols)
    back_rows = lax.all_to_all(returned, ("ctx", "seq"), split_axis=0, concat_axis=0, tiled=True)
    back_rows = back_rows.reshape(owners * slot_count, local_cols)
    token_grads = lax.dot_general(
        membership.astype(jnp.bfloat16),
        back_rows,
        (((0,), (0,)), ((), ())),
        preferred_element_type=jnp.float32,
    )
    return token_grads.astype(jnp.bfloat16)


BF16 = jnp.bfloat16
F32 = jnp.float32
MESH = pl.DeviceIdType.MESH
EDGE = 8


def mm(a, b):
    return jnp.dot(a, b, preferred_element_type=F32)


def fused_kernel(
    Z, Y, H, q_ref, k_ref, v_ref, res_ref, gain_ref, w_ref, proj_ref, tgt_ref, idr_ref, idc_ref,
    out_ref,
    kbuf, vbuf, attbuf, wbuf, wnat, projbuf, resbuf, s1, r1, s2, r2, nbuf, ssbuf, sst, ssall,
    psend, pbuf, idbuf, tsend, tbuf, ebuf, edge_prev, edge_next,
    send_sem, recv_sem, res_send, res_recv, up_send, down_send, att_recv, home_send, p_recv, ss_recv,
):
    z, y, h = lax.axis_index("ctx"), lax.axis_index("seq"), lax.axis_index("head")
    core, xpos = h % 2, h // 2
    mate = h + 1 - 2 * core
    cross = (h + 2) % H
    other_y = 1 - y
    owners = Z * Y
    me = z * Y + y
    T = q_ref.shape[0]
    F = gain_ref.shape[1] // Z
    half, quarter = T // 2, T // 4

    barrier = pltpu.get_barrier_semaphore()
    count = 0
    for dz in range(Z):
        for dh in range(H):
            if dz or dh:
                pl.semaphore_signal(
                    barrier, inc=1, device_id=((z + dz) % Z, y, (h + dh) % H), device_id_type=MESH
                )
                count += 1
        pl.semaphore_signal(
            barrier, inc=1, device_id=((z + dz) % Z, other_y, h), device_id_type=MESH
        )
        count += 1
    pl.semaphore_wait(barrier, count)

    sends = []

    def send(source, dest, device):
        n = len(sends)
        copy = pltpu.make_async_remote_copy(
            src_ref=source, dst_ref=dest, send_sem=send_sem.at[n], recv_sem=recv_sem.at[n],
            device_id=device, device_id_type=MESH,
        )
        copy.start()
        sends.append(copy)
        return copy

    def owner(step):
        block = (me + step + owners) % owners
        return (block // Y, block % Y, h)

    def rows_of(head):
        return pl.multiple_of((head % 2) * half + (head // 2) * quarter, 16)

    halo = []
    for step in range(1, STOPS + 1):
        halo.append(send(k_ref, kbuf.at[STOPS - step], owner(step)))
        halo.append(send(v_ref, vbuf.at[STOPS - step], owner(step)))
    ids_in = [send(idr_ref, idbuf.at[k], owner(k)) for k in range(1, owners)]

    wrows = w_ref.shape[0] // Z

    def w_chunk(block):
        return w_ref.at[pl.ds(pl.multiple_of(block * wrows, 16), wrows)]

    w_z = [send(w_chunk((z + m) % Z), wbuf.at[me], ((z + m) % Z, y, h)) for m in range(1, Z)]
    w_y = [send(w_chunk(z), wbuf.at[me], (z, other_y, h))]
    wbuf[me] = w_chunk(z)[...]

    res_copies = []
    for n in range(H):
        hh = (h + n) % H
        copy = pltpu.make_async_remote_copy(
            src_ref=res_ref.at[pl.ds(rows_of(hh), quarter)], dst_ref=resbuf.at[z],
            send_sem=res_send.at[n], recv_sem=res_recv.at[z],
            device_id=(h, y, hh), device_id_type=MESH,
        )
        res_copies.append(copy)

    local = pltpu.make_async_copy(
        res_ref.at[pl.ds(rows_of(h), quarter)], resbuf.at[z], res_recv.at[z]
    )

    slots = tbuf.shape[1]
    students = tgt_ref.shape[0]
    shift = owners.bit_length() - 1

    def choose():
        for k in range(1, owners):
            ids_in[k - 1].wait_recv()
        slot = lax.broadcasted_iota(jnp.int32, (slots, students), 0)
        row = lax.broadcasted_iota(jnp.int32, (slots, students), 1)
        for k in range(owners):
            ids = idr_ref[0:1, 0:1] if k == 0 else idbuf[k, 0:1, 0:1]
            dist = row * owners + me - ids
            pick = ((dist >= slot * owners) & (dist < slot * owners + owners)).astype(F32)
            rows = mm(pick.astype(BF16), tgt_ref[...]).astype(BF16)
            if k == 0:
                tbuf[0] = rows
            else:
                tsend[k] = rows
        return [send(tsend.at[k], tbuf.at[k], owner(-k)) for k in range(1, owners)]


    for copy in halo:
        copy.wait_recv()
    keys = jnp.concatenate([kbuf[s] for s in range(STOPS)] + [k_ref[...]], axis=0)
    values = jnp.concatenate([vbuf[s] for s in range(STOPS)] + [v_ref[...]], axis=0)
    span = (STOPS + 1) * T
    qpos = lax.broadcasted_iota(jnp.int32, (T, span), 0) + STOPS * T
    kpos = lax.broadcasted_iota(jnp.int32, (T, span), 1)
    visible = (kpos <= qpos) & (kpos > qpos - WIN) & (kpos >= (STOPS - me) * T)
    for g in range(q_ref.shape[1] // HD):
        scores = lax.dot_general(
            q_ref[:, g * HD:(g + 1) * HD], keys, (((1,), (1,)), ((), ())),
            preferred_element_type=F32,
        ) * HD ** (-0.5)
        scores = jnp.where(visible, scores, -1e30)
        exponent = jnp.exp(scores - jnp.max(scores, axis=-1, keepdims=True))
        inverse = 1.0 / jnp.sum(exponent, axis=-1, keepdims=True)
        attbuf[z, :, g * HD:(g + 1) * HD] = mm((exponent * inverse).astype(BF16), values).astype(BF16)

    far = z // (Z // 2)

    def near(m):
        base = z + far * (Z - 1 - 2 * z)
        slot = 1 - base if m == 1 else (base if m == 0 else base * 0 + m)
        return slot + far * (Z - 1 - 2 * slot)

    def along(slot, up):
        sems = up_send if up else down_send
        return pltpu.make_async_remote_copy(
            src_ref=attbuf.at[slot], dst_ref=attbuf.at[slot], send_sem=sems.at[slot],
            recv_sem=att_recv.at[slot], device_id=(z + 1 if up else z - 1, y, h),
            device_id_type=MESH,
        )

    def each_way(slot, act):
        @pl.when((slot <= z) & (z < Z - 1))
        def _():
            act(along(slot, True))

        @pl.when((slot >= z) & (z > 0))
        def _():
            act(along(slot, False))

    def relay(m):
        slot = near(m)
        pltpu.make_async_copy(attbuf.at[slot], attbuf.at[slot], att_recv.at[slot]).wait()
        each_way(slot, lambda copy: copy.start())

    for m in range(1, Z):
        w_z[m - 1].wait_recv()
        slot = ((z - m + Z) % Z) * Y + y
        w_y.append(send(wbuf.at[slot], wbuf.at[slot], (z, other_y, h)))
    each_way(z, lambda copy: copy.start())
    proj_in = send(proj_ref, projbuf.at[y], (z, other_y, h))
    projbuf[y] = proj_ref[...]
    for n in range(1, H):
        res_copies[n].start()

    @pl.when(z != h)
    def _():
        res_copies[0].start()

    @pl.when(z == h)
    def _():
        local.start()

    for copy in w_y:
        copy.wait_recv()

    group = 128 // owners
    r_io = lax.broadcasted_iota(jnp.int32, (128, 128), 0)
    c_io = lax.broadcasted_iota(jnp.int32, (128, 128), 1)
    place = ((r_io & (group - 1)) * owners + (r_io >> (group.bit_length() - 1)) == c_io).astype(F32).astype(BF16)
    for k in range(F // 128):
        rows = jnp.concatenate([wbuf[o, k * group:(k + 1) * group] for o in range(owners)], axis=0)
        wnat[:, k * 128:(k + 1) * 128] = lax.dot_general(
            rows, place, (((0,), (0,)), ((), ())), preferred_element_type=F32
        ).astype(BF16)

    gain = gain_ref[:, pl.ds(pl.multiple_of(z * F, 128), F)]
    mine, his = pl.multiple_of(core * half, 16), pl.multiple_of((1 - core) * half, 16)
    own_quarter = pl.multiple_of(xpos * quarter, 16)
    his_quarter = pl.multiple_of((1 - xpos) * quarter, 16)
    at_mine = rows_of(h)
    at_cross = rows_of(cross)
    first, second, third, mates, ss_in, p_in = [], [], [], [], [], []

    def homeward(source, dest, m, sems, kind):
        copy = pltpu.make_async_remote_copy(
            src_ref=source, dst_ref=dest, send_sem=home_send.at[kind, m], recv_sem=sems.at[z],
            device_id=(near(m), y, h), device_id_type=MESH,
        )
        copy.start()
        return copy

    def stage_a(m):
        source = attbuf.at[near(m)]
        s1[m] = mm(source[pl.ds(his, half)], wnat[...]).astype(BF16)
        first.append(send(s1.at[m], r1.at[m], (z, y, mate)))

    def stage_b(m):
        source = attbuf.at[near(m)]
        mine_a = mm(source[pl.ds(pl.multiple_of(mine + his_quarter, 16), quarter)], wnat[...])
        first[m].wait_recv()
        s2[m] = (mine_a + r1[m, pl.ds(his_quarter, quarter)].astype(F32)).astype(BF16)
        second.append(send(s2.at[m], r2.at[m], (z, y, cross)))

    def stage_c(m):
        source = attbuf.at[near(m)]
        total = mm(source[pl.ds(at_mine, quarter)], wnat[...])
        total = total + r1[m, pl.ds(own_quarter, quarter)].astype(F32)
        origin = near(m)
        pltpu.make_async_copy(resbuf.at[origin], resbuf.at[origin], res_recv.at[origin]).wait()
        second[m].wait_recv()
        total = total + r2[m].astype(F32) + resbuf[origin].astype(F32)
        nbuf[m, pl.ds(at_mine, quarter)] = (total * gain).astype(BF16)
        block = nbuf.at[m, pl.ds(at_mine, quarter)]
        third.append(send(block, block, (z, y, cross)))
        mates.append([send(block, block, (z, y, mate))])
        squares = jnp.sum(total * total, axis=1, keepdims=True)
        squares = jnp.broadcast_to(squares, (quarter, 128))
        if m == 0:
            ssbuf[z] = squares
        else:
            sst[m] = squares
            ss_in.append(homeward(sst.at[m], ssbuf.at[z], m, ss_recv, 0))

    def stage_d(m):
        third[m].wait_recv()
        block = nbuf.at[m, pl.ds(at_cross, quarter)]
        mates[m].append(send(block, block, (z, y, mate)))

    def stage_e(m):
        for copy in mates[m]:
            copy.wait_recv()
        if m == 0:
            proj_in.wait_recv()
        depth = F // Y
        part = mm(nbuf[m, :, 0:depth], projbuf[0])
        for s in range(1, Y):
            part = part + mm(nbuf[m, :, s * depth:(s + 1) * depth], projbuf[s])
        if m == 0:
            ebuf[...] = part
        else:
            psend[m] = part.astype(BF16)
            p_in.append(homeward(psend.at[m], pbuf.at[z], m, p_recv, 1))

    stage_a(0)
    stage_b(0)
    stage_c(0)
    relay(1)
    stage_a(1)
    stage_d(0)
    stage_b(1)
    stage_e(0)
    stage_c(1)
    relay(2)
    stage_a(2)
    stage_d(1)
    stage_b(2)
    stage_e(1)
    stage_c(2)
    relay(3)
    targets_in = choose()
    stage_a(3)
    stage_d(2)
    stage_b(3)
    stage_e(2)
    stage_c(3)

    squares = ssbuf[z]
    for m in range(1, Z):
        origin = near(m)
        pltpu.make_async_copy(ssbuf.at[origin], ssbuf.at[origin], ss_recv.at[origin]).wait()
        squares = squares + ssbuf[origin]
    ssall[pl.ds(at_mine, quarter)] = squares
    block = ssall.at[pl.ds(at_mine, quarter)]
    ss_all = [send(block, block, (z, y, (h + n) % H)) for n in range(1, H)]
    stage_d(3)
    stage_e(3)
    for copy in ss_all:
        copy.wait_recv()
    projected = ebuf[...]
    for m in range(1, Z):
        origin = near(m)
        pltpu.make_async_copy(pbuf.at[origin], pbuf.at[origin], p_recv.at[origin]).wait()
        projected = projected + pbuf[origin].astype(F32)
    projected = projected * lax.rsqrt(ssall[:, 0:1] / D + EPSILON)
    ebuf[...] = projected
    after = send(ebuf.at[pl.ds(T - EDGE, EDGE)], edge_prev, owner(1))
    before = send(ebuf.at[pl.ds(0, EDGE)], edge_next, owner(-1))

    ids = idc_ref[...]
    same = (ids == idr_ref[0:1, :]).astype(F32)
    sums = jnp.dot(
        same, projected, precision=lax.Precision.HIGHEST, preferred_element_type=F32
    )
    counts = jnp.sum(same, axis=1, keepdims=True)
    for copy in targets_in:
        copy.wait_recv()
    start = idr_ref[0:1, 0:1]
    from_owner = ((ids & (owners - 1)) - me + owners) & (owners - 1)
    column = from_owner * slots + ((ids - start) >> shift)
    choice = (
        lax.broadcasted_iota(jnp.int32, (T, owners * slots), 1) == column
    ).astype(F32).astype(BF16)
    wanted = mm(choice, jnp.concatenate([tbuf[k] for k in range(owners)], axis=0))
    after.wait_recv()
    before.wait_recv()
    for u in range(MOST - 1):
        spot = EDGE - 1 - u
        hit = (ids == idbuf[1, 0:1, T - 1 - u:T - u]).astype(F32)
        sums = sums + hit * edge_prev[spot:spot + 1]
        counts = counts + hit
        hit = (ids == idbuf[owners - 1, 0:1, u:u + 1]).astype(F32)
        sums = sums + hit * edge_next[u:u + 1]
        counts = counts + hit
    out_ref[...] = ((sums / counts - wanted) / counts).astype(BF16)

    for copy in sends:
        copy.wait_send()
    for copy in ss_in + p_in:
        copy.wait_send()
    for slot in range(Z):
        each_way(slot, lambda copy: copy.wait_send())
    for n in range(1, H):
        res_copies[n].wait_send()

    @pl.when(z != h)
    def _():
        res_copies[0].wait_send()


MOST = 3


def fused(
    sizes, queries, key_rows, value_rows, residual, norm_gain, w_out, student_proj, target, span_ids
):
    Z, Y, H = sizes
    owners = Z * Y
    T, width = queries.shape
    kv = key_rows.shape[1]
    F = residual.shape[1]
    cols = student_proj.shape[1]
    w = w_out.reshape(w_out.shape[0], w_out.shape[2])
    tgt = target.reshape(target.shape[0], target.shape[2])
    half, quarter = T // 2, T // 4
    slots = -(-(-(-T // owners)) // 16) * 16
    n_copies = 96
    ids_rows = jnp.broadcast_to(span_ids[None, :], (8, T))
    vmem = pltpu.VMEM
    call = pl.pallas_call(
        functools.partial(fused_kernel, Z, Y, H),
        out_shape=jax.ShapeDtypeStruct((T, cols), BF16),
        in_specs=[pl.BlockSpec(memory_space=pltpu.VMEM)] * 10,
        out_specs=pl.BlockSpec(memory_space=pltpu.VMEM),
        scratch_shapes=[
            vmem((STOPS, T, kv), BF16),
            vmem((STOPS, T, kv), BF16),
            vmem((Z, T, width), BF16),
            vmem((owners, w.shape[0] // Z, width), BF16),
            vmem((width, F), BF16),
            vmem((Y, student_proj.shape[0], cols), BF16),
            vmem((Z, quarter, F), BF16),
            vmem((Z, half, F), BF16),
            vmem((Z, half, F), BF16),
            vmem((Z, quarter, F), BF16),
            vmem((Z, quarter, F), BF16),
            vmem((Z, T, F), BF16),
            vmem((Z, quarter, 128), F32),
            vmem((Z, quarter, 128), F32),
            vmem((T, 128), F32),
            vmem((Z, T, cols), BF16),
            vmem((Z, T, cols), BF16),
            vmem((owners, 8, T), jnp.int32),
            vmem((owners, slots, cols), BF16),
            vmem((owners, slots, cols), BF16),
            vmem((T, cols), F32),
            vmem((EDGE, cols), F32),
            vmem((EDGE, cols), F32),
            pltpu.SemaphoreType.DMA((n_copies,)),
            pltpu.SemaphoreType.DMA((n_copies,)),
            pltpu.SemaphoreType.DMA((H,)),
            pltpu.SemaphoreType.DMA((Z,)),
            pltpu.SemaphoreType.DMA((Z,)),
            pltpu.SemaphoreType.DMA((Z,)),
            pltpu.SemaphoreType.DMA((Z,)),
            pltpu.SemaphoreType.DMA((2, Z)),
            pltpu.SemaphoreType.DMA((Z,)),
            pltpu.SemaphoreType.DMA((Z,)),
        ],
        compiler_params=pltpu.CompilerParams(
            collective_id=0, has_side_effects=True, vmem_limit_bytes=60 * 2**20
        ),
        name="layer",
    )
    return call(
        queries, key_rows, value_rows, residual, norm_gain.reshape(1, -1), w, student_proj, tgt,
        ids_rows, span_ids[:, None],
    )


def solution(mesh):
    sizes = tuple(mesh.shape[axis] for axis in ("ctx", "seq", "head"))
    owners = sizes[0] * sizes[1]
    small = sizes[1] == 2 and sizes[0] == 4 and sizes[2] == 4
    body = functools.partial(fused, sizes) if small else per_device
    return jax.shard_map(
        body,
        mesh=mesh,
        in_specs=(
            P(("ctx", "seq"), "head"),
            P(("ctx", "seq"), "head"),
            P(("ctx", "seq"), "head"),
            P(("ctx", "seq"), "head"),
            P(),
            P(None, ("ctx", "seq"), "head"),
            P(("ctx", "seq"), "head"),
            P(None, ("ctx", "seq"), "head"),
            P(("ctx", "seq")),
        ),
        out_specs=P(("ctx", "seq"), "head"),
        check_vma=False,
    )
```

```python
import functools

import jax
import jax.numpy as jnp
from jax import lax
from jax.experimental import pallas as pl
from jax.experimental.pallas import tpu as pltpu
from jax.sharding import PartitionSpec as P

D = 5120
HD = 128
STOPS = 2
WIN = 384


EPSILON = 1e-06


def passed_along(value, axis, steps):
    count = lax.axis_size(axis)
    first, last = (max(0, -steps), min(count, count - steps))
    return lax.ppermute(value, axis, [(source, source + steps) for source in range(first, last)])


def attend(queries, keys_all, values_all, query_pos, key_pos):
    tok_rows = queries.shape[0]
    kv_heads = keys_all.shape[1] // HD
    group_size = queries.shape[1] // HD // kv_heads
    query_blocks = queries.reshape(tok_rows, kv_heads, group_size, HD)
    key_blocks = keys_all.reshape(keys_all.shape[0], kv_heads, HD)
    value_blocks = values_all.reshape(values_all.shape[0], kv_heads, HD)
    scores = jnp.einsum(
        "qhgd,khd->hgqk", query_blocks, key_blocks, preferred_element_type=jnp.float32
    ) * HD ** (-0.5)
    visible = (
        (key_pos[None, :] <= query_pos[:, None])
        & (key_pos[None, :] > query_pos[:, None] - WIN)
        & (key_pos[None, :] >= 0)
    )
    scores = jnp.where(visible, scores, -1e30)
    largest = jnp.max(scores, axis=-1, keepdims=True)
    exponent = jnp.exp(scores - largest)
    probabilities = (exponent / jnp.sum(exponent, axis=-1, keepdims=True)).astype(jnp.bfloat16)
    attended = jnp.einsum(
        "hgqk,khd->qhgd", probabilities, value_blocks, preferred_element_type=jnp.float32
    )
    return attended.reshape(tok_rows, -1).astype(jnp.bfloat16)


def per_device(
    queries, key_rows, value_rows, residual, norm_gain, w_out, student_proj, target, span_ids
):
    tok_rows = queries.shape[0]
    block_index = lax.axis_index(("ctx", "seq"))
    owners = lax.axis_size(("ctx", "seq"))
    stacked = jnp.stack([key_rows, value_rows])
    arrived = []
    moving = stacked
    for back_step in range(STOPS):
        moving = passed_along(moving, ("ctx", "seq"), 1)
        arrived.append(moving)
    ordered = jnp.concatenate(arrived[::-1] + [stacked], axis=1)
    query_pos = block_index * tok_rows + jnp.arange(tok_rows, dtype=jnp.int32)
    key_pos = (block_index - STOPS) * tok_rows + jnp.arange((STOPS + 1) * tok_rows, dtype=jnp.int32)
    attended = attend(queries, ordered[0], ordered[1], query_pos, key_pos)
    w_source = lax.all_to_all(w_out, "head", split_axis=0, concat_axis=2, tiled=True)
    w_slab, p_slab = (
        lax.all_gather(w_source, ("ctx", "seq"), axis=1, tiled=True),
        lax.all_gather(student_proj, ("ctx", "seq"), axis=0, tiled=True),
    )
    w_slab = w_slab.reshape(-1, w_slab.shape[2])
    col_width = residual.shape[1]
    col_offset = lax.axis_index("head") * col_width
    gain_cols = lax.dynamic_slice_in_dim(norm_gain, col_offset, col_width, 0)
    all_heads = lax.all_gather(attended, "head", axis=1, tiled=True)
    share_cols = lax.dot_general(
        all_heads, w_slab, (((1,), (1,)), ((), ())), preferred_element_type=jnp.float32
    ) + residual.astype(jnp.float32)
    squares = lax.psum(jnp.sum(share_cols * share_cols, axis=1), "head")
    scaled = (share_cols * lax.rsqrt(squares / D + EPSILON)[:, None] * gain_cols[None, :]).astype(
        jnp.bfloat16
    )
    normed = lax.all_gather(scaled, "head", axis=1, tiled=True)
    projected = jnp.dot(normed, p_slab, preferred_element_type=jnp.float32)
    first_id = span_ids[0]
    slot_count = -(-tok_rows // owners)
    owner_iota = lax.broadcasted_iota(jnp.int32, (owners, slot_count), 0)
    slot_iota = lax.broadcasted_iota(jnp.int32, (owners, slot_count), 1)
    slot_ids = first_id + (owner_iota - first_id) % owners + slot_iota * owners
    slot_flat = slot_ids.reshape(-1)
    membership = (slot_flat[:, None] == span_ids[None, :]).astype(jnp.float32)
    pooled = jnp.dot(
        membership, projected, precision=lax.Precision.HIGHEST, preferred_element_type=jnp.float32
    )
    token_counts = jnp.sum(membership, axis=1)
    target_rows = (slot_flat // owners).astype(jnp.float32)
    local_cols = projected.shape[1]
    pooled_send = pooled.reshape(owners, slot_count, local_cols)
    counts_send = token_counts.reshape(owners, slot_count)
    rows_send = target_rows.reshape(owners, slot_count)
    got_sums, got_counts, got_rows = (
        lax.all_to_all(
            pooled_send.astype(jnp.bfloat16),
            ("ctx", "seq"),
            split_axis=0,
            concat_axis=0,
            tiled=True,
        ).astype(pooled_send.dtype),
        lax.all_to_all(
            counts_send.astype(jnp.bfloat16),
            ("ctx", "seq"),
            split_axis=0,
            concat_axis=0,
            tiled=True,
        ).astype(counts_send.dtype),
        lax.all_to_all(
            rows_send.astype(jnp.bfloat16), ("ctx", "seq"), split_axis=0, concat_axis=0, tiled=True
        ).astype(rows_send.dtype),
    )
    stu_rows = target.shape[0]
    row_iota = jnp.arange(stu_rows, dtype=jnp.float32)
    assign = (got_rows.reshape(-1)[None, :] == row_iota[:, None]).astype(jnp.float32)
    span_sums = jnp.dot(
        assign,
        got_sums.reshape(owners * slot_count, local_cols),
        precision=lax.Precision.HIGHEST,
        preferred_element_type=jnp.float32,
    )
    span_counts = jnp.dot(
        assign,
        got_counts.reshape(-1),
        precision=lax.Precision.HIGHEST,
        preferred_element_type=jnp.float32,
    )
    pooled_mean = span_sums / span_counts[:, None]
    grad_rows = ((pooled_mean - target[:, 0, :].astype(jnp.float32)) / span_counts[:, None]).astype(
        jnp.bfloat16
    )
    returned = lax.dot_general(
        assign.astype(jnp.bfloat16),
        grad_rows,
        (((0,), (0,)), ((), ())),
        preferred_element_type=jnp.float32,
    ).astype(jnp.bfloat16)
    returned = returned.reshape(owners, slot_count, local_cols)
    back_rows = lax.all_to_all(returned, ("ctx", "seq"), split_axis=0, concat_axis=0, tiled=True)
    back_rows = back_rows.reshape(owners * slot_count, local_cols)
    token_grads = lax.dot_general(
        membership.astype(jnp.bfloat16),
        back_rows,
        (((0,), (0,)), ((), ())),
        preferred_element_type=jnp.float32,
    )
    return token_grads.astype(jnp.bfloat16)


BF16 = jnp.bfloat16
F32 = jnp.float32
MESH = pl.DeviceIdType.MESH
EDGE = 8


def mm(a, b):
    return jnp.dot(a, b, preferred_element_type=F32)


def fused_kernel(
    Z, Y, H, q_ref, k_ref, v_ref, res_ref, gain_ref, w_ref, proj_ref, tgt_ref, idr_ref, idc_ref,
    out_ref,
    kbuf, vbuf, attbuf, wbuf, wnat, projbuf, resbuf, s1, r1, s2, r2, nbuf, ssbuf, sst, ssall,
    psend, pbuf, idbuf, tsend, tbuf, ebuf, edge_prev, edge_next,
    send_sem, recv_sem, res_send, res_recv, up_send, down_send, att_recv, home_send, p_recv, ss_recv, w_send, w_recv,
):
    z, y, h = lax.axis_index("ctx"), lax.axis_index("seq"), lax.axis_index("head")
    core, xpos = h % 2, h // 2
    mate = h + 1 - 2 * core
    cross = (h + 2) % H
    other_y = 1 - y
    owners = Z * Y
    me = z * Y + y
    T = q_ref.shape[0]
    F = gain_ref.shape[1] // Z
    half, quarter = T // 2, T // 4

    barrier = pltpu.get_barrier_semaphore()
    count = 0
    for dz in range(Z):
        for dh in range(H):
            if dz or dh:
                pl.semaphore_signal(
                    barrier, inc=1, device_id=((z + dz) % Z, y, (h + dh) % H), device_id_type=MESH
                )
                count += 1
        pl.semaphore_signal(
            barrier, inc=1, device_id=((z + dz) % Z, other_y, h), device_id_type=MESH
        )
        count += 1
    pl.semaphore_wait(barrier, count)

    sends = []

    def send(source, dest, device):
        n = len(sends)
        copy = pltpu.make_async_remote_copy(
            src_ref=source, dst_ref=dest, send_sem=send_sem.at[n], recv_sem=recv_sem.at[n],
            device_id=device, device_id_type=MESH,
        )
        copy.start()
        sends.append(copy)
        return copy

    def owner(step):
        block = (me + step + owners) % owners
        return (block // Y, block % Y, h)

    def rows_of(head):
        return pl.multiple_of((head % 2) * half + (head // 2) * quarter, 16)

    halo = []
    for step in range(1, STOPS + 1):
        halo.append(send(k_ref, kbuf.at[STOPS - step], owner(step)))
        halo.append(send(v_ref, vbuf.at[STOPS - step], owner(step)))
    ids_in = [send(idr_ref, idbuf.at[k], owner(k)) for k in range(1, owners)]

    wrows = w_ref.shape[0] // Z

    def w_chunk(block):
        return w_ref.at[pl.ds(pl.multiple_of(block * wrows, 16), wrows)]

    far = z // (Z // 2)

    def near(m):
        base = z + far * (Z - 1 - 2 * z)
        slot = 1 - base if m == 1 else (base if m == 0 else base * 0 + m)
        return slot + far * (Z - 1 - 2 * slot)

    w_z = []
    for m in range(1, Z):
        copy = pltpu.make_async_remote_copy(
            src_ref=w_chunk(near(m)), dst_ref=wbuf.at[me], send_sem=w_send.at[m],
            recv_sem=w_recv.at[z], device_id=(near(m), y, h), device_id_type=MESH,
        )
        copy.start()
        w_z.append(copy)
    w_y = [send(w_chunk(z), wbuf.at[me], (z, other_y, h))]
    wbuf[me] = w_chunk(z)[...]
    prows = proj_ref.shape[0] // 4
    proj_in = []

    def send_proj(begin, stop):
        rows = slice(begin * prows, stop * prows)
        proj_in.append(send(proj_ref.at[rows], projbuf.at[y, rows], (z, other_y, h)))

    send_proj(0, 2)

    res_copies = []
    for n in range(H):
        hh = (h + n) % H
        copy = pltpu.make_async_remote_copy(
            src_ref=res_ref.at[pl.ds(rows_of(hh), quarter)], dst_ref=resbuf.at[z],
            send_sem=res_send.at[n], recv_sem=res_recv.at[z],
            device_id=(h, y, hh), device_id_type=MESH,
        )
        res_copies.append(copy)

    local = pltpu.make_async_copy(
        res_ref.at[pl.ds(rows_of(h), quarter)], resbuf.at[z], res_recv.at[z]
    )

    slots = tbuf.shape[1]
    students = tgt_ref.shape[0]
    shift = owners.bit_length() - 1

    def choose():
        for k in range(1, owners):
            ids_in[k - 1].wait_recv()
        slot = lax.broadcasted_iota(jnp.int32, (slots, students), 0)
        row = lax.broadcasted_iota(jnp.int32, (slots, students), 1)
        for k in range(owners):
            ids = idr_ref[0:1, 0:1] if k == 0 else idbuf[k, 0:1, 0:1]
            dist = row * owners + me - ids
            pick = ((dist >= slot * owners) & (dist < slot * owners + owners)).astype(F32)
            rows = mm(pick.astype(BF16), tgt_ref[...]).astype(BF16)
            if k == 0:
                tbuf[0] = rows
            else:
                tsend[k] = rows
        return [send(tsend.at[k], tbuf.at[k], owner(-k)) for k in range(1, owners)]


    for copy in halo:
        copy.wait_recv()
    keys = jnp.concatenate([kbuf[s] for s in range(STOPS)] + [k_ref[...]], axis=0)
    values = jnp.concatenate([vbuf[s] for s in range(STOPS)] + [v_ref[...]], axis=0)
    span = (STOPS + 1) * T
    qpos = lax.broadcasted_iota(jnp.int32, (T, span), 0) + STOPS * T
    kpos = lax.broadcasted_iota(jnp.int32, (T, span), 1)
    visible = (kpos <= qpos) & (kpos > qpos - WIN) & (kpos >= (STOPS - me) * T)
    for g in range(q_ref.shape[1] // HD):
        scores = lax.dot_general(
            q_ref[:, g * HD:(g + 1) * HD], keys, (((1,), (1,)), ((), ())),
            preferred_element_type=F32,
        ) * HD ** (-0.5)
        scores = jnp.where(visible, scores, -1e30)
        exponent = jnp.exp(scores - jnp.max(scores, axis=-1, keepdims=True))
        inverse = 1.0 / jnp.sum(exponent, axis=-1, keepdims=True)
        attbuf[z, :, g * HD:(g + 1) * HD] = mm((exponent * inverse).astype(BF16), values).astype(BF16)

    def along(slot, up):
        sems = up_send if up else down_send
        return pltpu.make_async_remote_copy(
            src_ref=attbuf.at[slot], dst_ref=attbuf.at[slot], send_sem=sems.at[slot],
            recv_sem=att_recv.at[slot], device_id=(z + 1 if up else z - 1, y, h),
            device_id_type=MESH,
        )

    def each_way(slot, act):
        @pl.when((slot <= z) & (z < Z - 1))
        def _():
            act(along(slot, True))

        @pl.when((slot >= z) & (z > 0))
        def _():
            act(along(slot, False))

    def relay(m):
        slot = near(m)
        pltpu.make_async_copy(attbuf.at[slot], attbuf.at[slot], att_recv.at[slot]).wait()
        each_way(slot, lambda copy: copy.start())

    @pl.when(z == h)
    def _():
        local.start()
        for n in range(1, H):
            res_copies[n].start()

    for m in range(1, Z):
        origin = near(m)
        slot = origin * Y + y
        pltpu.make_async_copy(wbuf.at[slot], wbuf.at[slot], w_recv.at[origin]).wait()
        w_y.append(send(wbuf.at[slot], wbuf.at[slot], (z, other_y, h)))
        if m == 1:
            send_proj(2, 3)
    each_way(z, lambda copy: copy.start())
    projbuf[y] = proj_ref[...]
    middle = (z > 0) & (z < Z - 1)
    end = (z == 0) | (z == Z - 1)

    @pl.when(middle)
    def _():
        relay(1)

    @pl.when(z != h)
    def _():
        for n in range(H):
            res_copies[n].start()

    @pl.when(middle)
    def _():
        relay(2)

    for copy in w_y:
        copy.wait_recv()
    send_proj(3, 4)

    group = 128 // owners
    r_io = lax.broadcasted_iota(jnp.int32, (128, 128), 0)
    c_io = lax.broadcasted_iota(jnp.int32, (128, 128), 1)
    place = ((r_io & (group - 1)) * owners + (r_io >> (group.bit_length() - 1)) == c_io).astype(F32).astype(BF16)
    for k in range(F // 128):
        rows = jnp.concatenate([wbuf[o, k * group:(k + 1) * group] for o in range(owners)], axis=0)
        wnat[:, k * 128:(k + 1) * 128] = lax.dot_general(
            rows, place, (((0,), (0,)), ((), ())), preferred_element_type=F32
        ).astype(BF16)

    gain = gain_ref[:, pl.ds(pl.multiple_of(z * F, 128), F)]
    mine, his = pl.multiple_of(core * half, 16), pl.multiple_of((1 - core) * half, 16)
    own_quarter = pl.multiple_of(xpos * quarter, 16)
    his_quarter = pl.multiple_of((1 - xpos) * quarter, 16)
    at_mine = rows_of(h)
    at_cross = rows_of(cross)
    first, second, third, mates, ss_in, p_in = [], [], [], [], [], []

    def homeward(source, dest, m, sems, kind):
        copy = pltpu.make_async_remote_copy(
            src_ref=source, dst_ref=dest, send_sem=home_send.at[kind, m], recv_sem=sems.at[z],
            device_id=(near(m), y, h), device_id_type=MESH,
        )
        copy.start()
        return copy

    def stage_a(m):
        source = attbuf.at[near(m)]
        s1[m] = mm(source[pl.ds(his, half)], wnat[...]).astype(BF16)
        first.append(send(s1.at[m], r1.at[m], (z, y, mate)))

    def stage_b(m):
        source = attbuf.at[near(m)]
        mine_a = mm(source[pl.ds(pl.multiple_of(mine + his_quarter, 16), quarter)], wnat[...])
        first[m].wait_recv()
        s2[m] = (mine_a + r1[m, pl.ds(his_quarter, quarter)].astype(F32)).astype(BF16)
        second.append(send(s2.at[m], r2.at[m], (z, y, cross)))

    def stage_c(m):
        source = attbuf.at[near(m)]
        total = mm(source[pl.ds(at_mine, quarter)], wnat[...])
        total = total + r1[m, pl.ds(own_quarter, quarter)].astype(F32)
        origin = near(m)
        pltpu.make_async_copy(resbuf.at[origin], resbuf.at[origin], res_recv.at[origin]).wait()
        second[m].wait_recv()
        total = total + r2[m].astype(F32) + resbuf[origin].astype(F32)
        nbuf[m, pl.ds(at_mine, quarter)] = (total * gain).astype(BF16)
        block = nbuf.at[m, pl.ds(at_mine, quarter)]
        third.append(send(block, block, (z, y, cross)))
        mates.append([send(block, block, (z, y, mate))])
        squares = jnp.sum(total * total, axis=1, keepdims=True)
        squares = jnp.broadcast_to(squares, (quarter, 128))
        if m == 0:
            ssbuf[z] = squares
        else:
            sst[m] = squares
            ss_in.append(homeward(sst.at[m], ssbuf.at[z], m, ss_recv, 0))

    def stage_d(m):
        third[m].wait_recv()
        block = nbuf.at[m, pl.ds(at_cross, quarter)]
        mates[m].append(send(block, block, (z, y, mate)))

    def stage_e(m):
        for copy in mates[m]:
            copy.wait_recv()
        if m == 0:
            for copy in proj_in:
                copy.wait_recv()
        depth = F // Y
        part = mm(nbuf[m, :, 0:depth], projbuf[0])
        for s in range(1, Y):
            part = part + mm(nbuf[m, :, s * depth:(s + 1) * depth], projbuf[s])
        if m == 0:
            ebuf[...] = part
        else:
            psend[m] = part.astype(BF16)
            p_in.append(homeward(psend.at[m], pbuf.at[z], m, p_recv, 1))

    stage_a(0)
    stage_b(0)

    @pl.when(end)
    def _():
        relay(1)

    stage_a(1)
    stage_b(1)
    stage_c(0)

    @pl.when(middle)
    def _():
        relay(3)

    targets_in = choose()
    stage_d(0)
    stage_c(1)

    @pl.when(end)
    def _():
        relay(2)

    stage_a(2)
    stage_e(0)
    stage_b(2)
    stage_d(1)

    @pl.when(end)
    def _():
        relay(3)

    stage_a(3)
    stage_c(2)
    stage_e(1)
    stage_b(3)
    stage_d(2)
    stage_c(3)
    stage_e(2)

    squares = ssbuf[z]
    for m in range(1, Z):
        origin = near(m)
        pltpu.make_async_copy(ssbuf.at[origin], ssbuf.at[origin], ss_recv.at[origin]).wait()
        squares = squares + ssbuf[origin]
    ssall[pl.ds(at_mine, quarter)] = squares
    block = ssall.at[pl.ds(at_mine, quarter)]
    ss_all = [send(block, block, (z, y, (h + n) % H)) for n in range(1, H)]
    stage_d(3)
    stage_e(3)
    for copy in ss_all:
        copy.wait_recv()
    projected = ebuf[...]
    for m in range(1, Z):
        origin = near(m)
        pltpu.make_async_copy(pbuf.at[origin], pbuf.at[origin], p_recv.at[origin]).wait()
        projected = projected + pbuf[origin].astype(F32)
    projected = projected * lax.rsqrt(ssall[:, 0:1] / D + EPSILON)
    ebuf[...] = projected
    after = send(ebuf.at[pl.ds(T - EDGE, EDGE)], edge_prev, owner(1))
    before = send(ebuf.at[pl.ds(0, EDGE)], edge_next, owner(-1))

    ids = idc_ref[...]
    same = (ids == idr_ref[0:1, :]).astype(F32)
    sums = jnp.dot(
        same, projected, precision=lax.Precision.HIGHEST, preferred_element_type=F32
    )
    counts = jnp.sum(same, axis=1, keepdims=True)
    for copy in targets_in:
        copy.wait_recv()
    start = idr_ref[0:1, 0:1]
    from_owner = ((ids & (owners - 1)) - me + owners) & (owners - 1)
    column = from_owner * slots + ((ids - start) >> shift)
    choice = (
        lax.broadcasted_iota(jnp.int32, (T, owners * slots), 1) == column
    ).astype(F32).astype(BF16)
    wanted = mm(choice, jnp.concatenate([tbuf[k] for k in range(owners)], axis=0))
    after.wait_recv()
    before.wait_recv()
    for u in range(MOST - 1):
        spot = EDGE - 1 - u
        hit = (ids == idbuf[1, 0:1, T - 1 - u:T - u]).astype(F32)
        sums = sums + hit * edge_prev[spot:spot + 1]
        counts = counts + hit
        hit = (ids == idbuf[owners - 1, 0:1, u:u + 1]).astype(F32)
        sums = sums + hit * edge_next[u:u + 1]
        counts = counts + hit
    out_ref[...] = ((sums / counts - wanted) / counts).astype(BF16)

    for copy in sends:
        copy.wait_send()
    for copy in ss_in + p_in + w_z:
        copy.wait_send()
    for slot in range(Z):
        each_way(slot, lambda copy: copy.wait_send())
    for n in range(1, H):
        res_copies[n].wait_send()

    @pl.when(z != h)
    def _():
        res_copies[0].wait_send()


MOST = 3


def fused(
    sizes, queries, key_rows, value_rows, residual, norm_gain, w_out, student_proj, target, span_ids
):
    Z, Y, H = sizes
    owners = Z * Y
    T, width = queries.shape
    kv = key_rows.shape[1]
    F = residual.shape[1]
    cols = student_proj.shape[1]
    w = w_out.reshape(w_out.shape[0], w_out.shape[2])
    tgt = target.reshape(target.shape[0], target.shape[2])
    half, quarter = T // 2, T // 4
    slots = -(-(-(-T // owners)) // 16) * 16
    n_copies = 96
    ids_rows = jnp.broadcast_to(span_ids[None, :], (8, T))
    vmem = pltpu.VMEM
    call = pl.pallas_call(
        functools.partial(fused_kernel, Z, Y, H),
        out_shape=jax.ShapeDtypeStruct((T, cols), BF16),
        in_specs=[pl.BlockSpec(memory_space=pltpu.VMEM)] * 10,
        out_specs=pl.BlockSpec(memory_space=pltpu.VMEM),
        scratch_shapes=[
            vmem((STOPS, T, kv), BF16),
            vmem((STOPS, T, kv), BF16),
            vmem((Z, T, width), BF16),
            vmem((owners, w.shape[0] // Z, width), BF16),
            vmem((width, F), BF16),
            vmem((Y, student_proj.shape[0], cols), BF16),
            vmem((Z, quarter, F), BF16),
            vmem((Z, half, F), BF16),
            vmem((Z, half, F), BF16),
            vmem((Z, quarter, F), BF16),
            vmem((Z, quarter, F), BF16),
            vmem((Z, T, F), BF16),
            vmem((Z, quarter, 128), F32),
            vmem((Z, quarter, 128), F32),
            vmem((T, 128), F32),
            vmem((Z, T, cols), BF16),
            vmem((Z, T, cols), BF16),
            vmem((owners, 8, T), jnp.int32),
            vmem((owners, slots, cols), BF16),
            vmem((owners, slots, cols), BF16),
            vmem((T, cols), F32),
            vmem((EDGE, cols), F32),
            vmem((EDGE, cols), F32),
            pltpu.SemaphoreType.DMA((n_copies,)),
            pltpu.SemaphoreType.DMA((n_copies,)),
            pltpu.SemaphoreType.DMA((H,)),
            pltpu.SemaphoreType.DMA((Z,)),
            pltpu.SemaphoreType.DMA((Z,)),
            pltpu.SemaphoreType.DMA((Z,)),
            pltpu.SemaphoreType.DMA((Z,)),
            pltpu.SemaphoreType.DMA((2, Z)),
            pltpu.SemaphoreType.DMA((Z,)),
            pltpu.SemaphoreType.DMA((Z,)),
            pltpu.SemaphoreType.DMA((Z,)),
            pltpu.SemaphoreType.DMA((Z,)),
        ],
        compiler_params=pltpu.CompilerParams(
            collective_id=0, has_side_effects=True, vmem_limit_bytes=60 * 2**20
        ),
        name="layer",
    )
    return call(
        queries, key_rows, value_rows, residual, norm_gain.reshape(1, -1), w, student_proj, tgt,
        ids_rows, span_ids[:, None],
    )


def solution(mesh):
    sizes = tuple(mesh.shape[axis] for axis in ("ctx", "seq", "head"))
    owners = sizes[0] * sizes[1]
    small = sizes[1] == 2 and sizes[0] == 4 and sizes[2] == 4
    body = functools.partial(fused, sizes) if small else per_device
    return jax.shard_map(
        body,
        mesh=mesh,
        in_specs=(
            P(("ctx", "seq"), "head"),
            P(("ctx", "seq"), "head"),
            P(("ctx", "seq"), "head"),
            P(("ctx", "seq"), "head"),
            P(),
            P(None, ("ctx", "seq"), "head"),
            P(("ctx", "seq"), "head"),
            P(None, ("ctx", "seq"), "head"),
            P(("ctx", "seq")),
        ),
        out_specs=P(("ctx", "seq"), "head"),
        check_vma=False,
    )
```

```python
import functools

import jax
import jax.numpy as jnp
from jax import lax
from jax.experimental import pallas as pl
from jax.experimental.pallas import tpu as pltpu
from jax.sharding import PartitionSpec as P

D = 5120
HD = 128
STOPS = 2
WIN = 384


EPSILON = 1e-06


def passed_along(value, axis, steps):
    count = lax.axis_size(axis)
    first, last = (max(0, -steps), min(count, count - steps))
    return lax.ppermute(value, axis, [(source, source + steps) for source in range(first, last)])


def attend(queries, keys_all, values_all, query_pos, key_pos):
    tok_rows = queries.shape[0]
    kv_heads = keys_all.shape[1] // HD
    group_size = queries.shape[1] // HD // kv_heads
    query_blocks = queries.reshape(tok_rows, kv_heads, group_size, HD)
    key_blocks = keys_all.reshape(keys_all.shape[0], kv_heads, HD)
    value_blocks = values_all.reshape(values_all.shape[0], kv_heads, HD)
    scores = jnp.einsum(
        "qhgd,khd->hgqk", query_blocks, key_blocks, preferred_element_type=jnp.float32
    ) * HD ** (-0.5)
    visible = (
        (key_pos[None, :] <= query_pos[:, None])
        & (key_pos[None, :] > query_pos[:, None] - WIN)
        & (key_pos[None, :] >= 0)
    )
    scores = jnp.where(visible, scores, -1e30)
    largest = jnp.max(scores, axis=-1, keepdims=True)
    exponent = jnp.exp(scores - largest)
    probabilities = (exponent / jnp.sum(exponent, axis=-1, keepdims=True)).astype(jnp.bfloat16)
    attended = jnp.einsum(
        "hgqk,khd->qhgd", probabilities, value_blocks, preferred_element_type=jnp.float32
    )
    return attended.reshape(tok_rows, -1).astype(jnp.bfloat16)


def per_device(
    queries, key_rows, value_rows, residual, norm_gain, w_out, student_proj, target, span_ids
):
    tok_rows = queries.shape[0]
    block_index = lax.axis_index(("ctx", "seq"))
    owners = lax.axis_size(("ctx", "seq"))
    stacked = jnp.stack([key_rows, value_rows])
    arrived = []
    moving = stacked
    for back_step in range(STOPS):
        moving = passed_along(moving, ("ctx", "seq"), 1)
        arrived.append(moving)
    ordered = jnp.concatenate(arrived[::-1] + [stacked], axis=1)
    query_pos = block_index * tok_rows + jnp.arange(tok_rows, dtype=jnp.int32)
    key_pos = (block_index - STOPS) * tok_rows + jnp.arange((STOPS + 1) * tok_rows, dtype=jnp.int32)
    attended = attend(queries, ordered[0], ordered[1], query_pos, key_pos)
    w_source = lax.all_to_all(w_out, "head", split_axis=0, concat_axis=2, tiled=True)
    w_slab, p_slab = (
        lax.all_gather(w_source, ("ctx", "seq"), axis=1, tiled=True),
        lax.all_gather(student_proj, ("ctx", "seq"), axis=0, tiled=True),
    )
    w_slab = w_slab.reshape(-1, w_slab.shape[2])
    col_width = residual.shape[1]
    col_offset = lax.axis_index("head") * col_width
    gain_cols = lax.dynamic_slice_in_dim(norm_gain, col_offset, col_width, 0)
    all_heads = lax.all_gather(attended, "head", axis=1, tiled=True)
    share_cols = lax.dot_general(
        all_heads, w_slab, (((1,), (1,)), ((), ())), preferred_element_type=jnp.float32
    ) + residual.astype(jnp.float32)
    squares = lax.psum(jnp.sum(share_cols * share_cols, axis=1), "head")
    scaled = (share_cols * lax.rsqrt(squares / D + EPSILON)[:, None] * gain_cols[None, :]).astype(
        jnp.bfloat16
    )
    normed = lax.all_gather(scaled, "head", axis=1, tiled=True)
    projected = jnp.dot(normed, p_slab, preferred_element_type=jnp.float32)
    first_id = span_ids[0]
    slot_count = -(-tok_rows // owners)
    owner_iota = lax.broadcasted_iota(jnp.int32, (owners, slot_count), 0)
    slot_iota = lax.broadcasted_iota(jnp.int32, (owners, slot_count), 1)
    slot_ids = first_id + (owner_iota - first_id) % owners + slot_iota * owners
    slot_flat = slot_ids.reshape(-1)
    membership = (slot_flat[:, None] == span_ids[None, :]).astype(jnp.float32)
    pooled = jnp.dot(
        membership, projected, precision=lax.Precision.HIGHEST, preferred_element_type=jnp.float32
    )
    token_counts = jnp.sum(membership, axis=1)
    target_rows = (slot_flat // owners).astype(jnp.float32)
    local_cols = projected.shape[1]
    pooled_send = pooled.reshape(owners, slot_count, local_cols)
    counts_send = token_counts.reshape(owners, slot_count)
    rows_send = target_rows.reshape(owners, slot_count)
    got_sums, got_counts, got_rows = (
        lax.all_to_all(
            pooled_send.astype(jnp.bfloat16),
            ("ctx", "seq"),
            split_axis=0,
            concat_axis=0,
            tiled=True,
        ).astype(pooled_send.dtype),
        lax.all_to_all(
            counts_send.astype(jnp.bfloat16),
            ("ctx", "seq"),
            split_axis=0,
            concat_axis=0,
            tiled=True,
        ).astype(counts_send.dtype),
        lax.all_to_all(
            rows_send.astype(jnp.bfloat16), ("ctx", "seq"), split_axis=0, concat_axis=0, tiled=True
        ).astype(rows_send.dtype),
    )
    stu_rows = target.shape[0]
    row_iota = jnp.arange(stu_rows, dtype=jnp.float32)
    assign = (got_rows.reshape(-1)[None, :] == row_iota[:, None]).astype(jnp.float32)
    span_sums = jnp.dot(
        assign,
        got_sums.reshape(owners * slot_count, local_cols),
        precision=lax.Precision.HIGHEST,
        preferred_element_type=jnp.float32,
    )
    span_counts = jnp.dot(
        assign,
        got_counts.reshape(-1),
        precision=lax.Precision.HIGHEST,
        preferred_element_type=jnp.float32,
    )
    pooled_mean = span_sums / span_counts[:, None]
    grad_rows = ((pooled_mean - target[:, 0, :].astype(jnp.float32)) / span_counts[:, None]).astype(
        jnp.bfloat16
    )
    returned = lax.dot_general(
        assign.astype(jnp.bfloat16),
        grad_rows,
        (((0,), (0,)), ((), ())),
        preferred_element_type=jnp.float32,
    ).astype(jnp.bfloat16)
    returned = returned.reshape(owners, slot_count, local_cols)
    back_rows = lax.all_to_all(returned, ("ctx", "seq"), split_axis=0, concat_axis=0, tiled=True)
    back_rows = back_rows.reshape(owners * slot_count, local_cols)
    token_grads = lax.dot_general(
        membership.astype(jnp.bfloat16),
        back_rows,
        (((0,), (0,)), ((), ())),
        preferred_element_type=jnp.float32,
    )
    return token_grads.astype(jnp.bfloat16)


BF16 = jnp.bfloat16
F32 = jnp.float32
MESH = pl.DeviceIdType.MESH
EDGE = 8


def mm(a, b):
    return jnp.dot(a, b, preferred_element_type=F32)


def fused_kernel(
    Z, Y, H, q_ref, k_ref, v_ref, res_ref, gain_ref, w_ref, proj_ref, tgt_ref, idr_ref, idc_ref,
    out_ref,
    kbuf, vbuf, attbuf, wbuf, wnat, projbuf, resbuf, s1, r1, s2, r2, nbuf, ssbuf, sst, ssall,
    psend, pbuf, idbuf, tsend, tbuf, ebuf, edge_prev, edge_next,
    send_sem, recv_sem, res_send, res_recv, up_send, down_send, att_recv, home_send, p_recv, ss_recv, w_send, w_recv,
    edge_send, edge_recv,
):
    z, y, h = lax.axis_index("ctx"), lax.axis_index("seq"), lax.axis_index("head")
    core, xpos = h % 2, h // 2
    mate = h + 1 - 2 * core
    cross = (h + 2) % H
    other_y = 1 - y
    owners = Z * Y
    me = z * Y + y
    T = q_ref.shape[0]
    F = gain_ref.shape[1] // Z
    half, quarter = T // 2, T // 4

    barrier = pltpu.get_barrier_semaphore()
    count = 0
    for dz in range(Z):
        for dh in range(H):
            if dz or dh:
                pl.semaphore_signal(
                    barrier, inc=1, device_id=((z + dz) % Z, y, (h + dh) % H), device_id_type=MESH
                )
                count += 1
        pl.semaphore_signal(
            barrier, inc=1, device_id=((z + dz) % Z, other_y, h), device_id_type=MESH
        )
        count += 1
    pl.semaphore_wait(barrier, count)

    sends = []

    def send(source, dest, device):
        n = len(sends)
        copy = pltpu.make_async_remote_copy(
            src_ref=source, dst_ref=dest, send_sem=send_sem.at[n], recv_sem=recv_sem.at[n],
            device_id=device, device_id_type=MESH,
        )
        copy.start()
        sends.append(copy)
        return copy

    def owner(step):
        block = (me + step + owners) % owners
        return (block // Y, block % Y, h)

    def rows_of(head):
        return pl.multiple_of((head % 2) * half + (head // 2) * quarter, 16)

    halo = []
    for step in range(1, STOPS + 1):
        halo.append(send(k_ref, kbuf.at[STOPS - step], owner(step)))
        halo.append(send(v_ref, vbuf.at[STOPS - step], owner(step)))
    ids_in = [send(idr_ref, idbuf.at[k], owner(k)) for k in range(1, owners)]

    wrows = w_ref.shape[0] // Z

    def w_chunk(block):
        return w_ref.at[pl.ds(pl.multiple_of(block * wrows, 16), wrows)]

    far = z // (Z // 2)

    def near(m):
        base = z + far * (Z - 1 - 2 * z)
        slot = 1 - base if m == 1 else (base if m == 0 else base * 0 + m)
        return slot + far * (Z - 1 - 2 * slot)

    w_z = []
    for m in range(1, Z):
        copy = pltpu.make_async_remote_copy(
            src_ref=w_chunk(near(m)), dst_ref=wbuf.at[me], send_sem=w_send.at[m],
            recv_sem=w_recv.at[z], device_id=(near(m), y, h), device_id_type=MESH,
        )
        copy.start()
        w_z.append(copy)
    w_y = [send(w_chunk(z), wbuf.at[me], (z, other_y, h))]
    wbuf[me] = w_chunk(z)[...]
    prows = proj_ref.shape[0] // 4
    proj_in = []

    def send_proj(begin, stop):
        rows = slice(begin * prows, stop * prows)
        proj_in.append(send(proj_ref.at[rows], projbuf.at[y, rows], (z, other_y, h)))

    send_proj(0, 2)

    res_copies = []
    for n in range(H):
        hh = (h + n) % H
        copy = pltpu.make_async_remote_copy(
            src_ref=res_ref.at[pl.ds(rows_of(hh), quarter)], dst_ref=resbuf.at[z],
            send_sem=res_send.at[n], recv_sem=res_recv.at[z],
            device_id=(h, y, hh), device_id_type=MESH,
        )
        res_copies.append(copy)

    local = pltpu.make_async_copy(
        res_ref.at[pl.ds(rows_of(h), quarter)], resbuf.at[z], res_recv.at[z]
    )

    slots = tbuf.shape[1]
    students = tgt_ref.shape[0]
    shift = owners.bit_length() - 1

    def choose():
        for k in range(1, owners):
            ids_in[k - 1].wait_recv()
        slot = lax.broadcasted_iota(jnp.int32, (slots, students), 0)
        row = lax.broadcasted_iota(jnp.int32, (slots, students), 1)
        for k in range(owners):
            ids = idr_ref[0:1, 0:1] if k == 0 else idbuf[k, 0:1, 0:1]
            dist = row * owners + me - ids
            pick = ((dist >= slot * owners) & (dist < slot * owners + owners)).astype(F32)
            rows = mm(pick.astype(BF16), tgt_ref[...]).astype(BF16)
            if k == 0:
                tbuf[0] = rows
            else:
                tsend[k] = rows
        return [send(tsend.at[k], tbuf.at[k], owner(-k)) for k in range(1, owners)]


    for copy in halo:
        copy.wait_recv()
    keys = jnp.concatenate([kbuf[s] for s in range(STOPS)] + [k_ref[...]], axis=0)
    values = jnp.concatenate([vbuf[s] for s in range(STOPS)] + [v_ref[...]], axis=0)
    span = (STOPS + 1) * T
    qpos = lax.broadcasted_iota(jnp.int32, (T, span), 0) + STOPS * T
    kpos = lax.broadcasted_iota(jnp.int32, (T, span), 1)
    visible = (kpos <= qpos) & (kpos > qpos - WIN) & (kpos >= (STOPS - me) * T)
    for g in range(q_ref.shape[1] // HD):
        scores = lax.dot_general(
            q_ref[:, g * HD:(g + 1) * HD], keys, (((1,), (1,)), ((), ())),
            preferred_element_type=F32,
        ) * HD ** (-0.5)
        scores = jnp.where(visible, scores, -1e30)
        exponent = jnp.exp(scores - jnp.max(scores, axis=-1, keepdims=True))
        inverse = 1.0 / jnp.sum(exponent, axis=-1, keepdims=True)
        attbuf[z, :, g * HD:(g + 1) * HD] = mm((exponent * inverse).astype(BF16), values).astype(BF16)

    def along(slot, up):
        sems = up_send if up else down_send
        return pltpu.make_async_remote_copy(
            src_ref=attbuf.at[slot], dst_ref=attbuf.at[slot], send_sem=sems.at[slot],
            recv_sem=att_recv.at[slot], device_id=(z + 1 if up else z - 1, y, h),
            device_id_type=MESH,
        )

    def each_way(slot, act):
        @pl.when((slot <= z) & (z < Z - 1))
        def _():
            act(along(slot, True))

        @pl.when((slot >= z) & (z > 0))
        def _():
            act(along(slot, False))

    def relay(m):
        slot = near(m)
        pltpu.make_async_copy(attbuf.at[slot], attbuf.at[slot], att_recv.at[slot]).wait()
        each_way(slot, lambda copy: copy.start())

    @pl.when(z == h)
    def _():
        local.start()
        for n in range(1, H):
            res_copies[n].start()

    for m in range(1, Z):
        origin = near(m)
        slot = origin * Y + y
        pltpu.make_async_copy(wbuf.at[slot], wbuf.at[slot], w_recv.at[origin]).wait()
        w_y.append(send(wbuf.at[slot], wbuf.at[slot], (z, other_y, h)))
        if m == 1:
            send_proj(2, 3)
    each_way(z, lambda copy: copy.start())
    projbuf[y] = proj_ref[...]
    middle = (z > 0) & (z < Z - 1)
    end = (z == 0) | (z == Z - 1)

    @pl.when(middle)
    def _():
        relay(1)

    @pl.when(z != h)
    def _():
        for n in range(H):
            res_copies[n].start()

    @pl.when(middle)
    def _():
        relay(2)

    for copy in w_y:
        copy.wait_recv()
    send_proj(3, 4)

    group = 128 // owners
    r_io = lax.broadcasted_iota(jnp.int32, (128, 128), 0)
    c_io = lax.broadcasted_iota(jnp.int32, (128, 128), 1)
    place = ((r_io & (group - 1)) * owners + (r_io >> (group.bit_length() - 1)) == c_io).astype(F32).astype(BF16)
    for k in range(F // 128):
        rows = jnp.concatenate([wbuf[o, k * group:(k + 1) * group] for o in range(owners)], axis=0)
        wnat[:, k * 128:(k + 1) * 128] = lax.dot_general(
            rows, place, (((0,), (0,)), ((), ())), preferred_element_type=F32
        ).astype(BF16)

    gain = gain_ref[:, pl.ds(pl.multiple_of(z * F, 128), F)]
    mine, his = pl.multiple_of(core * half, 16), pl.multiple_of((1 - core) * half, 16)
    own_quarter = pl.multiple_of(xpos * quarter, 16)
    his_quarter = pl.multiple_of((1 - xpos) * quarter, 16)
    at_mine = rows_of(h)
    at_cross = rows_of(cross)
    first, second, third, mates, ss_in, p_in = [], [], [], [], [], []

    def homeward(source, dest, m, sems, kind):
        copy = pltpu.make_async_remote_copy(
            src_ref=source, dst_ref=dest, send_sem=home_send.at[kind, m], recv_sem=sems.at[z],
            device_id=(near(m), y, h), device_id_type=MESH,
        )
        copy.start()
        return copy

    def stage_a(m):
        source = attbuf.at[near(m)]
        s1[m] = mm(source[pl.ds(his, half)], wnat[...]).astype(BF16)
        first.append(send(s1.at[m], r1.at[m], (z, y, mate)))

    def stage_b(m):
        source = attbuf.at[near(m)]
        mine_a = mm(source[pl.ds(pl.multiple_of(mine + his_quarter, 16), quarter)], wnat[...])
        first[m].wait_recv()
        s2[m] = (mine_a + r1[m, pl.ds(his_quarter, quarter)].astype(F32)).astype(BF16)
        second.append(send(s2.at[m], r2.at[m], (z, y, cross)))

    def stage_c(m):
        source = attbuf.at[near(m)]
        total = mm(source[pl.ds(at_mine, quarter)], wnat[...])
        total = total + r1[m, pl.ds(own_quarter, quarter)].astype(F32)
        origin = near(m)
        pltpu.make_async_copy(resbuf.at[origin], resbuf.at[origin], res_recv.at[origin]).wait()
        second[m].wait_recv()
        total = total + r2[m].astype(F32) + resbuf[origin].astype(F32)
        nbuf[m, pl.ds(at_mine, quarter)] = (total * gain).astype(BF16)
        block = nbuf.at[m, pl.ds(at_mine, quarter)]
        third.append(send(block, block, (z, y, cross)))
        mates.append([send(block, block, (z, y, mate))])
        squares = jnp.sum(total * total, axis=1, keepdims=True)
        squares = jnp.broadcast_to(squares, (quarter, 128))
        if m == 0:
            ssbuf[z] = squares
        else:
            sst[m] = squares
            ss_in.append(homeward(sst.at[m], ssbuf.at[z], m, ss_recv, 0))

    def stage_d(m):
        third[m].wait_recv()
        block = nbuf.at[m, pl.ds(at_cross, quarter)]
        mates[m].append(send(block, block, (z, y, mate)))

    def stage_e(m):
        for copy in mates[m]:
            copy.wait_recv()
        if m == 0:
            for copy in proj_in:
                copy.wait_recv()
        depth = F // Y
        part = mm(nbuf[m, :, 0:depth], projbuf[0])
        for s in range(1, Y):
            part = part + mm(nbuf[m, :, s * depth:(s + 1) * depth], projbuf[s])
        if m == 0:
            ebuf[...] = part
        else:
            psend[m] = part.astype(BF16)
            p_in.append(homeward(psend.at[m], pbuf.at[z], m, p_recv, 1))

    stage_a(0)
    stage_b(0)

    @pl.when(end)
    def _():
        relay(1)

    stage_a(1)
    stage_b(1)
    stage_c(0)

    @pl.when(middle)
    def _():
        relay(3)

    targets_in = choose()
    stage_d(0)
    stage_c(1)

    @pl.when(end)
    def _():
        relay(2)

    stage_a(2)
    stage_e(0)
    stage_b(2)
    stage_d(1)

    @pl.when(end)
    def _():
        relay(3)

    stage_a(3)
    stage_c(2)
    stage_e(1)
    stage_b(3)
    stage_d(2)
    stage_c(3)
    stage_e(2)

    squares = ssbuf[z]
    for m in range(1, Z):
        origin = near(m)
        pltpu.make_async_copy(ssbuf.at[origin], ssbuf.at[origin], ss_recv.at[origin]).wait()
        squares = squares + ssbuf[origin]
    ssall[pl.ds(at_mine, quarter)] = squares
    block = ssall.at[pl.ds(at_mine, quarter)]
    ss_all = [send(block, block, (z, y, (h + n) % H)) for n in range(1, H)]
    stage_d(3)
    stage_e(3)
    for copy in ss_all:
        copy.wait_recv()
    projected = ebuf[...]
    for m in range(1, Z):
        origin = near(m)
        pltpu.make_async_copy(pbuf.at[origin], pbuf.at[origin], p_recv.at[origin]).wait()
        projected = projected + pbuf[origin].astype(F32)
    projected = projected * lax.rsqrt(ssall[:, 0:1] / D + EPSILON)
    ebuf[...] = projected
    def edge(source, dest, device, n):
        return pltpu.make_async_remote_copy(
            src_ref=source, dst_ref=dest, send_sem=edge_send.at[n], recv_sem=edge_recv.at[n],
            device_id=device, device_id_type=MESH,
        )

    after = edge(ebuf.at[pl.ds(T - EDGE, EDGE)], edge_prev, owner(1), 0)
    before = edge(ebuf.at[pl.ds(0, EDGE)], edge_next, owner(-1), 1)
    has_prev, has_next = me > 0, me < owners - 1

    @pl.when(has_next)
    def _():
        after.start()

    @pl.when(has_prev)
    def _():
        before.start()

    @pl.when(me == 0)
    def _():
        edge_prev[...] = jnp.zeros_like(edge_prev)

    @pl.when(me == owners - 1)
    def _():
        edge_next[...] = jnp.zeros_like(edge_next)


    ids = idc_ref[...]
    same = (ids == idr_ref[0:1, :]).astype(F32)
    sums = jnp.dot(
        same, projected, precision=lax.Precision.HIGHEST, preferred_element_type=F32
    )
    counts = jnp.sum(same, axis=1, keepdims=True)
    for copy in targets_in:
        copy.wait_recv()
    start = idr_ref[0:1, 0:1]
    from_owner = ((ids & (owners - 1)) - me + owners) & (owners - 1)
    column = from_owner * slots + ((ids - start) >> shift)
    choice = (
        lax.broadcasted_iota(jnp.int32, (T, owners * slots), 1) == column
    ).astype(F32).astype(BF16)
    wanted = mm(choice, jnp.concatenate([tbuf[k] for k in range(owners)], axis=0))
    @pl.when(has_prev)
    def _():
        after.wait_recv()

    @pl.when(has_next)
    def _():
        before.wait_recv()

    for u in range(MOST - 1):
        spot = EDGE - 1 - u
        hit = (ids == idbuf[1, 0:1, T - 1 - u:T - u]).astype(F32)
        sums = sums + hit * edge_prev[spot:spot + 1]
        counts = counts + hit
        hit = (ids == idbuf[owners - 1, 0:1, u:u + 1]).astype(F32)
        sums = sums + hit * edge_next[u:u + 1]
        counts = counts + hit
    out_ref[...] = ((sums / counts - wanted) / counts).astype(BF16)

    for copy in sends:
        copy.wait_send()
    @pl.when(has_next)
    def _():
        after.wait_send()

    @pl.when(has_prev)
    def _():
        before.wait_send()

    for copy in ss_in + p_in + w_z:
        copy.wait_send()
    for slot in range(Z):
        each_way(slot, lambda copy: copy.wait_send())
    for n in range(1, H):
        res_copies[n].wait_send()

    @pl.when(z != h)
    def _():
        res_copies[0].wait_send()


MOST = 3


def fused(
    sizes, queries, key_rows, value_rows, residual, norm_gain, w_out, student_proj, target, span_ids
):
    Z, Y, H = sizes
    owners = Z * Y
    T, width = queries.shape
    kv = key_rows.shape[1]
    F = residual.shape[1]
    cols = student_proj.shape[1]
    w = w_out.reshape(w_out.shape[0], w_out.shape[2])
    tgt = target.reshape(target.shape[0], target.shape[2])
    half, quarter = T // 2, T // 4
    slots = -(-(-(-T // owners)) // 16) * 16
    n_copies = 96
    ids_rows = jnp.broadcast_to(span_ids[None, :], (8, T))
    vmem = pltpu.VMEM
    call = pl.pallas_call(
        functools.partial(fused_kernel, Z, Y, H),
        out_shape=jax.ShapeDtypeStruct((T, cols), BF16),
        in_specs=[pl.BlockSpec(memory_space=pltpu.VMEM)] * 10,
        out_specs=pl.BlockSpec(memory_space=pltpu.VMEM),
        scratch_shapes=[
            vmem((STOPS, T, kv), BF16),
            vmem((STOPS, T, kv), BF16),
            vmem((Z, T, width), BF16),
            vmem((owners, w.shape[0] // Z, width), BF16),
            vmem((width, F), BF16),
            vmem((Y, student_proj.shape[0], cols), BF16),
            vmem((Z, quarter, F), BF16),
            vmem((Z, half, F), BF16),
            vmem((Z, half, F), BF16),
            vmem((Z, quarter, F), BF16),
            vmem((Z, quarter, F), BF16),
            vmem((Z, T, F), BF16),
            vmem((Z, quarter, 128), F32),
            vmem((Z, quarter, 128), F32),
            vmem((T, 128), F32),
            vmem((Z, T, cols), BF16),
            vmem((Z, T, cols), BF16),
            vmem((owners, 8, T), jnp.int32),
            vmem((owners, slots, cols), BF16),
            vmem((owners, slots, cols), BF16),
            vmem((T, cols), F32),
            vmem((EDGE, cols), F32),
            vmem((EDGE, cols), F32),
            pltpu.SemaphoreType.DMA((n_copies,)),
            pltpu.SemaphoreType.DMA((n_copies,)),
            pltpu.SemaphoreType.DMA((H,)),
            pltpu.SemaphoreType.DMA((Z,)),
            pltpu.SemaphoreType.DMA((Z,)),
            pltpu.SemaphoreType.DMA((Z,)),
            pltpu.SemaphoreType.DMA((Z,)),
            pltpu.SemaphoreType.DMA((2, Z)),
            pltpu.SemaphoreType.DMA((Z,)),
            pltpu.SemaphoreType.DMA((Z,)),
            pltpu.SemaphoreType.DMA((Z,)),
            pltpu.SemaphoreType.DMA((Z,)),
            pltpu.SemaphoreType.DMA((2,)),
            pltpu.SemaphoreType.DMA((2,)),
        ],
        compiler_params=pltpu.CompilerParams(
            collective_id=0, has_side_effects=True, vmem_limit_bytes=60 * 2**20
        ),
        name="layer",
    )
    return call(
        queries, key_rows, value_rows, residual, norm_gain.reshape(1, -1), w, student_proj, tgt,
        ids_rows, span_ids[:, None],
    )


def solution(mesh):
    sizes = tuple(mesh.shape[axis] for axis in ("ctx", "seq", "head"))
    owners = sizes[0] * sizes[1]
    small = sizes[1] == 2 and sizes[0] == 4 and sizes[2] == 4
    body = functools.partial(fused, sizes) if small else per_device
    return jax.shard_map(
        body,
        mesh=mesh,
        in_specs=(
            P(("ctx", "seq"), "head"),
            P(("ctx", "seq"), "head"),
            P(("ctx", "seq"), "head"),
            P(("ctx", "seq"), "head"),
            P(),
            P(None, ("ctx", "seq"), "head"),
            P(("ctx", "seq"), "head"),
            P(None, ("ctx", "seq"), "head"),
            P(("ctx", "seq")),
        ),
        out_specs=P(("ctx", "seq"), "head"),
        check_vma=False,
    )
```
